128 devices in a mesh: branch: 2 (over core), seq: 64 (over x, z, y).
Axes of the slice: x: 4, y: 4, z: 4, core: 2. Of those that a mesh axis runs over, the one named last changes fastest.
Arguments:
- hidden: bfloat16 [2, 49152, 1024], P('branch', 'seq')
- noisy_mel_state: float32 [100, 49152], P(None, 'seq'), may hold values from -6 to 6
- modulation: float32 [5, 1024], replicated, may hold values from -3 to 3
- feedforward_in_weight: bfloat16 [1024, 2048], replicated, may hold values from -0.1875 to 0.1875
- feedforward_in_bias: float32 [2048], replicated, may hold values from -1.75 to 1.75
- feedforward_out_weight: bfloat16 [2048, 1024], replicated, may hold values from -0.125 to 0.125
- feedforward_out_bias: float32 [1024], replicated, may hold values from -1.75 to 1.75
- mel_velocity_weight: bfloat16 [1024, 100], replicated, may hold values from -0.1875 to 0.1875
- mel_velocity_bias: float32 [100], replicated, may hold values from -3 to 3
- input_conv_weight: bfloat16 [700, 512], replicated, may hold values from -0.21875 to 0.21875
- input_conv_bias: float32 [512], replicated, may hold values from -1.75 to 1.75
- transposed_conv_weight: bfloat16 [4096, 512], replicated, may hold values from -0.1875 to 0.1875
- transposed_conv_bias: float32 [256], replicated, may hold values from -1.75 to 1.75
- snake_freq_first: float32 [256], replicated, may hold values from 0.5 to 3
- dilated_conv_weight: bfloat16 [768, 256], replicated, may hold values from -0.21875 to 0.21875
- dilated_conv_bias: float32 [256], replicated, may hold values from -1.75 to 1.75
- snake_freq_second: float32 [256], replicated, may hold values from 0.5 to 3
- second_conv_weight: bfloat16 [768, 256], replicated, may hold values from -0.21875 to 0.21875
- second_conv_bias: float32 [256], replicated, may hold values from -1.75 to 1.75
- frame_holder: int32 [49152], P('seq'), may hold values from 0 to 127, as said below
- frame_position: int32 [49152], P('seq'), may hold values from 0 to 767, as said below
- holder_utterance_length: int32 [128], replicated, may hold values from 1 to 768, as said below
Outputs:
- wave: bfloat16 [128, 256, 6144], P(('branch', 'seq'))
The draws below stay inside these ranges and needn't reach their ends.
Inputs may be any that keep to these rules, and one draw needn't show every extreme that they name: `frame_holder`: the frames form 128 utterances, each a run of consecutive frames; all frames of an utterance name one owner, and each owner is named by exactly one utterance. `frame_position`: A frame's position in its utterance, 0 at the utterance's first frame. `holder_utterance_length`: the number of frames that name the owner; every utterance has at least one frame.
All inputs are finite; a program needn't handle non-finite values.
Results may differ from the reference program's by a relative error of at most 0.015.
Values may be sent and summed in bfloat16 or wider, within the bound.
No kernel may reach another device: no remote copies, remote signals or barrier semaphores. Data moves between devices by JAX's collectives and lax.ppermute only.
A program may use at most 128 MiB of HBM per device.

```python
import math
import jax
import jax.numpy as jnp
from jax import lax

D = 1024
FF = 2048
BINS = 100
CH0 = 512
UPSAMPLED_CHANS = 256
UP = 8
KT = 16
KPRE = 7
DILATION_RATE = 3
NFE = 16
F_DEV = 768
FRAMES = 49152
OWNERS = 128
MOST = 768
N_SEQ = 64


def utterance_layout(key):
    base_key = jax.random.fold_in(key, 11)
    pick_key, order_key, mix_key = jax.random.split(base_key, 3)
    longest = jax.random.randint(pick_key, (), 0, OWNERS)
    spare_frames = FRAMES - MOST
    even_share = spare_frames // (OWNERS - 1)
    leftover = spare_frames % (OWNERS - 1)
    indices = jnp.arange(OWNERS)
    others_rank = indices - (indices > longest).astype(jnp.int32)
    lengths = jnp.where(indices == longest, MOST, even_share + (others_rank < leftover).astype(jnp.int32))
    for mix_step in range(8):
        pair_key, amount_key = jax.random.split(jax.random.fold_in(mix_key, mix_step))
        shuffled = jax.random.permutation(pair_key, OWNERS)
        first_of = shuffled[0::2]
        second_of = shuffled[1::2]
        blocked = (first_of == longest) | (second_of == longest)
        pair_sum = lengths[first_of] + lengths[second_of]
        low_bound = jnp.maximum(1, pair_sum - MOST)
        high_bound = jnp.minimum(MOST, pair_sum - 1)
        new_first = jax.random.randint(amount_key, first_of.shape, low_bound, high_bound + 1)
        new_first = jnp.where(blocked, lengths[first_of], new_first)
        lengths = lengths.at[first_of].set(new_first).at[second_of].set(pair_sum - new_first)
    starts = jnp.cumsum(lengths) - lengths
    assign = jax.random.permutation(order_key, OWNERS)
    positions = jnp.arange(FRAMES)
    utterance = jnp.sum((positions[:, None] >= starts[None, :]).astype(jnp.int32), axis=1) - 1
    owners_of = assign[utterance].astype(jnp.int32)
    offsets = (positions - starts[utterance]).astype(jnp.int32)
    owner_lengths = jnp.zeros((OWNERS,), jnp.int32).at[assign].set(lengths.astype(jnp.int32))
    return (owners_of, offsets, owner_lengths)


def draw_frame_holder(key, part):
    return utterance_layout(key)[0]


def draw_frame_position(key, part):
    return utterance_layout(key)[1]


def draw_holder_utterance_length(key, part):
    return utterance_layout(key)[2]


def draw_hidden(key, part):
    col_key, row_key, entry_key = jax.random.split(jax.random.fold_in(key, 3), 3)
    column_scale = jnp.exp(jax.random.uniform(col_key, (D,), minval=0.0, maxval=math.log(10.0)))
    row_scale = jnp.exp(jax.random.uniform(row_key, (2, FRAMES, 1), minval=math.log(0.5), maxval=math.log(2.0)))
    entries = jax.random.normal(entry_key, (2, FRAMES, D))
    return (0.3 * entries * column_scale * row_scale).astype(jnp.bfloat16)


def levels(stream_key, extent, cuts, smallest, high):
    def one(dim, blocks):
        heights = jax.random.uniform(jax.random.fold_in(jax.random.fold_in(stream_key, 6), dim), (blocks,), jnp.float32, smallest / len(cuts), high / len(cuts))
        return jnp.repeat(jnp.exp(heights), extent[dim] // blocks).reshape((-1,) + (1,) * (len(extent) - dim - 1))

    factor_of = one(*cuts[0])
    for cut in cuts[1:]:
        factor_of = factor_of * one(*cut)
    return factor_of


def gaussian(stream_key, extent, scale, bound, cuts=(), kind=jnp.bfloat16):
    array = scale * jax.random.normal(stream_key, extent, jnp.float32)
    if cuts:
        array = array * levels(stream_key, extent, cuts, -0.22, 0.18)
    return jnp.clip(array, -bound, bound).astype(kind)


def setup_inputs(seed: int = 0) -> dict:
    key_of = jax.random.split(jax.random.key(seed), 23)
    hidden = draw_hidden(jax.random.fold_in(key_of[22], 71), 0)
    noisy_mel_state = gaussian(key_of[1], (BINS, FRAMES), 1.0, 6.0, ((1, 64),), jnp.float32)
    modulation = gaussian(key_of[2], (5, D), 0.5, 3.0, (), jnp.float32)
    feedforward_in_weight = gaussian(key_of[3], (D, FF), D ** -0.5, 0.1875)
    feedforward_in_bias = gaussian(key_of[4], (FF,), 0.3, 1.75, (), jnp.float32)
    feedforward_out_weight = gaussian(key_of[5], (FF, D), FF ** -0.5, 0.125)
    feedforward_out_bias = gaussian(key_of[6], (D,), 0.3, 1.75, (), jnp.float32)
    mel_velocity_weight = gaussian(key_of[7], (D, BINS), D ** -0.5, 0.1875)
    mel_velocity_bias = gaussian(key_of[8], (BINS,), 0.5, 3.0, (), jnp.float32)
    input_conv_weight = gaussian(key_of[9], (KPRE * BINS, CH0), (KPRE * BINS) ** -0.5, 0.21875)
    input_conv_bias = gaussian(key_of[10], (CH0,), 0.3, 1.75, (), jnp.float32)
    transposed_conv_weight = gaussian(key_of[11], (KT * UPSAMPLED_CHANS, CH0), (2 * CH0) ** -0.5, 0.1875)
    transposed_conv_bias = gaussian(key_of[12], (UPSAMPLED_CHANS,), 0.3, 1.75, (), jnp.float32)
    snake_freq_first = jnp.clip(jnp.exp(jax.random.uniform(key_of[13], (UPSAMPLED_CHANS,), jnp.float32, math.log(0.5), math.log(3.0))), 0.5, 3.0)
    dilated_conv_weight = gaussian(key_of[14], (3 * UPSAMPLED_CHANS, UPSAMPLED_CHANS), (3 * UPSAMPLED_CHANS) ** -0.5, 0.21875)
    dilated_conv_bias = gaussian(key_of[15], (UPSAMPLED_CHANS,), 0.3, 1.75, (), jnp.float32)
    snake_freq_second = jnp.clip(jnp.exp(jax.random.uniform(key_of[16], (UPSAMPLED_CHANS,), jnp.float32, math.log(0.5), math.log(3.0))), 0.5, 3.0)
    second_conv_weight = gaussian(key_of[17], (3 * UPSAMPLED_CHANS, UPSAMPLED_CHANS), (3 * UPSAMPLED_CHANS) ** -0.5, 0.21875)
    second_conv_bias = gaussian(key_of[18], (UPSAMPLED_CHANS,), 0.3, 1.75, (), jnp.float32)
    frame_holder = draw_frame_holder(jax.random.fold_in(key_of[22], 71), 0)
    frame_position = draw_frame_position(jax.random.fold_in(key_of[22], 71), 0)
    holder_utterance_length = draw_holder_utterance_length(jax.random.fold_in(key_of[22], 71), 0)
    return dict(hidden=hidden, noisy_mel_state=noisy_mel_state, modulation=modulation, feedforward_in_weight=feedforward_in_weight, feedforward_in_bias=feedforward_in_bias, feedforward_out_weight=feedforward_out_weight, feedforward_out_bias=feedforward_out_bias, mel_velocity_weight=mel_velocity_weight, mel_velocity_bias=mel_velocity_bias, input_conv_weight=input_conv_weight, input_conv_bias=input_conv_bias, transposed_conv_weight=transposed_conv_weight, transposed_conv_bias=transposed_conv_bias, snake_freq_first=snake_freq_first, dilated_conv_weight=dilated_conv_weight, dilated_conv_bias=dilated_conv_bias, snake_freq_second=snake_freq_second, second_conv_weight=second_conv_weight, second_conv_bias=second_conv_bias, frame_holder=frame_holder, frame_position=frame_position, holder_utterance_length=holder_utterance_length)


GUIDE = 2.0

def layer_norm(row_block):
    row_mean = lax.optimization_barrier(jnp.mean(row_block, axis=-1, keepdims=True))
    centred = row_block - row_mean
    row_var = lax.optimization_barrier(jnp.mean(centred * centred, axis=-1, keepdims=True))
    return centred * lax.rsqrt(row_var + 1e-06)

def velocity(row_block, modulation, feedforward_in_weight, feedforward_in_bias, feedforward_out_weight, feedforward_out_bias, mel_velocity_weight, mel_velocity_bias):
    residual_in = row_block.astype(jnp.float32)
    normed = (layer_norm(residual_in) * (1.0 + modulation[1]) + modulation[0]).astype(jnp.bfloat16)
    inner_pre = jnp.dot(normed, feedforward_in_weight, preferred_element_type=jnp.float32) + feedforward_in_bias
    active = jax.nn.gelu(inner_pre, approximate=True).astype(jnp.bfloat16)
    back_proj = jnp.dot(active, feedforward_out_weight, preferred_element_type=jnp.float32) + feedforward_out_bias
    block_out = residual_in + modulation[2] * back_proj
    final_norm = (layer_norm(block_out) * (1.0 + modulation[4]) + modulation[3]).astype(jnp.bfloat16)
    speed = lax.dot_general(mel_velocity_weight, final_norm, (((0,), (1,)), ((), ())), preferred_element_type=jnp.float32)
    return speed + mel_velocity_bias[:, None]

def shifted(values, offset):
    pad_width = abs(offset)
    last_axis = values.ndim - 1
    pad_spec = [(0, 0)] * last_axis + [(pad_width, pad_width)]
    padded = jnp.pad(values, pad_spec)
    return lax.slice_in_dim(padded, pad_width + offset, pad_width + offset + values.shape[last_axis], axis=last_axis)

def snake(signal, alpha_vec):
    sine_part = jnp.sin(alpha_vec[:, None] * signal)
    return signal + sine_part * sine_part / alpha_vec[:, None]

def dilated_output(values, weight, bias_vec, spacing, keep_mask):
    stacked = jnp.concatenate([shifted(values, -spacing), values, shifted(values, spacing)], axis=0)
    conv_out = lax.dot_general(weight, stacked, (((0,), (0,)), ((), ())), preferred_element_type=jnp.float32)
    return jnp.where(keep_mask[None, :], conv_out + bias_vec[:, None], 0.0)

def vocoder_synthesize(holder_mel, utterance_frames_length, input_conv_weight, input_conv_bias, transposed_conv_weight, transposed_conv_bias, snake_freq_first, dilated_conv_weight, dilated_conv_bias, snake_freq_second, second_conv_weight, second_conv_bias):
    most_rows = holder_mel.shape[1]
    channels = transposed_conv_weight.shape[0] // KT
    frame_keep = jnp.arange(most_rows) < utterance_frames_length
    half_kernel = KPRE // 2
    tap_list = [shifted(holder_mel, tap_index - half_kernel) for tap_index in range(KPRE)]
    stacked = jnp.concatenate(tap_list, axis=0)
    pre_out = lax.dot_general(input_conv_weight, stacked, (((0,), (0,)), ((), ())), preferred_element_type=jnp.float32)
    pre_out = jnp.where(frame_keep[None, :], pre_out + input_conv_bias[:, None], 0.0).astype(jnp.bfloat16)
    phases = jnp.dot(transposed_conv_weight, pre_out, preferred_element_type=jnp.float32).reshape(KT, channels, most_rows)
    pad_up = UP // 2
    direct = phases[pad_up:pad_up + UP]
    early_part = shifted(phases[UP + pad_up:], -1)
    late_part = shifted(phases[:UP - pad_up], 1)
    phase_sum = direct + jnp.concatenate([early_part, late_part], axis=0)
    woven_out = jnp.transpose(phase_sum, (1, 2, 0)).reshape(channels, most_rows * UP) + transposed_conv_bias[:, None]
    sample_keep_mask = jnp.arange(most_rows * UP) < utterance_frames_length * UP
    upsampled = jnp.where(sample_keep_mask[None, :], woven_out, 0.0).astype(jnp.bfloat16)
    first_snake_output = snake(upsampled.astype(jnp.float32), snake_freq_first).astype(jnp.bfloat16)
    inner_convolved = dilated_output(first_snake_output, dilated_conv_weight, dilated_conv_bias, DILATION_RATE, sample_keep_mask)
    second_act = snake(inner_convolved, snake_freq_second).astype(jnp.bfloat16)
    outer_conv = dilated_output(second_act, second_conv_weight, second_conv_bias, 1, sample_keep_mask)
    return (upsampled.astype(jnp.float32) + outer_conv).astype(jnp.bfloat16)

def reference(hidden, noisy_mel_state, modulation, feedforward_in_weight, feedforward_in_bias, feedforward_out_weight, feedforward_out_bias, mel_velocity_weight, mel_velocity_bias, input_conv_weight, input_conv_bias, transposed_conv_weight, transposed_conv_bias, snake_freq_first, dilated_conv_weight, dilated_conv_bias, snake_freq_second, second_conv_weight, second_conv_bias, frame_holder, frame_position, holder_utterance_length):
    step_size = math.cos(0.5 * math.pi * (NFE - 1) / NFE)
    block_count = 2 * FRAMES // F_DEV
    grouped = hidden.reshape(block_count, F_DEV, D)

    def one_block(row_block):
        return velocity(row_block, modulation, feedforward_in_weight, feedforward_in_bias, feedforward_out_weight, feedforward_out_bias, mel_velocity_weight, mel_velocity_bias)
    speeds = lax.map(one_block, grouped)
    speeds = speeds.reshape(2, N_SEQ, BINS, F_DEV).transpose(0, 2, 1, 3).reshape(2, BINS, FRAMES)
    guided = (1.0 + GUIDE) * speeds[0] - GUIDE * speeds[1]
    refined = (noisy_mel_state + step_size * guided).astype(jnp.bfloat16)
    flat_slot = frame_holder.astype(jnp.int32) * MOST + frame_position.astype(jnp.int32)
    placed = jnp.zeros((BINS, OWNERS * MOST), jnp.bfloat16).at[:, flat_slot].set(refined)
    owned_all = placed.reshape(BINS, OWNERS, MOST).transpose(1, 0, 2)

    def one_owner(paired_element):
        return vocoder_synthesize(paired_element[0], paired_element[1], input_conv_weight, input_conv_bias, transposed_conv_weight, transposed_conv_bias, snake_freq_first, dilated_conv_weight, dilated_conv_bias, snake_freq_second, second_conv_weight, second_conv_bias)
    return lax.map(one_owner, (owned_all, holder_utterance_length))
```

```python
import math

import jax
import jax.numpy as jnp
from jax import lax
from jax.sharding import PartitionSpec as P

UP = 8
KT = 16
KPRE = 7
DILATION_RATE = 3
NFE = 16


GUIDE = 2.0
LANES = 128


def layer_norm(row_block):
    row_mean = jnp.mean(row_block, axis=-1, keepdims=True)
    centred = row_block - row_mean
    row_var = jnp.mean(centred * centred, axis=-1, keepdims=True)
    return centred * lax.rsqrt(row_var + 1e-06)


def velocity(
    row_block,
    modulation,
    feedforward_in_weight,
    feedforward_in_bias,
    feedforward_out_weight,
    feedforward_out_bias,
    mel_velocity_weight,
    mel_velocity_bias,
):
    residual_in = row_block.astype(jnp.float32)
    normed = (layer_norm(residual_in) * (1.0 + modulation[1]) + modulation[0]).astype(jnp.bfloat16)
    inner_pre = (
        jnp.dot(normed, feedforward_in_weight, preferred_element_type=jnp.float32)
        + feedforward_in_bias
    )
    active = jax.nn.gelu(inner_pre, approximate=True).astype(jnp.bfloat16)
    back_proj = (
        jnp.dot(active, feedforward_out_weight, preferred_element_type=jnp.float32)
        + feedforward_out_bias
    )
    block_out = residual_in + modulation[2] * back_proj
    final_norm = (layer_norm(block_out) * (1.0 + modulation[4]) + modulation[3]).astype(
        jnp.bfloat16
    )
    speed = jnp.dot(final_norm, mel_velocity_weight, preferred_element_type=jnp.float32)
    return speed + mel_velocity_bias


def shifted(values, offset):
    pad_width = abs(offset)
    last_axis = values.ndim - 1
    pad_spec = [(0, 0)] * last_axis + [(pad_width, pad_width)]
    padded = jnp.pad(values, pad_spec)
    return lax.slice_in_dim(
        padded, pad_width + offset, pad_width + offset + values.shape[last_axis], axis=last_axis
    )


def snake(signal, alpha_vec):
    sine_part = jnp.sin(alpha_vec[:, None] * signal)
    return signal + sine_part * sine_part / alpha_vec[:, None]


def dilated_output(values, weight, bias_vec, spacing, keep_mask):
    stacked = jnp.concatenate([shifted(values, -spacing), values, shifted(values, spacing)], axis=0)
    conv_out = lax.dot_general(
        weight, stacked, (((0,), (0,)), ((), ())), preferred_element_type=jnp.float32
    )
    return jnp.where(keep_mask[None, :], conv_out + bias_vec[:, None], 0.0)


def vocoder_synthesize(
    holder_mel,
    utterance_frames_length,
    input_conv_weight,
    input_conv_bias,
    transposed_conv_weight,
    transposed_conv_bias,
    snake_freq_first,
    dilated_conv_weight,
    dilated_conv_bias,
    snake_freq_second,
    second_conv_weight,
    second_conv_bias,
):
    most_rows = holder_mel.shape[1]
    channels = transposed_conv_weight.shape[0] // KT
    frame_keep = jnp.arange(most_rows) < utterance_frames_length
    half_kernel = KPRE // 2
    tap_list = [shifted(holder_mel, tap_index - half_kernel) for tap_index in range(KPRE)]
    stacked = jnp.concatenate(tap_list, axis=0)
    pre_out = lax.dot_general(
        input_conv_weight, stacked, (((0,), (0,)), ((), ())), preferred_element_type=jnp.float32
    )
    pre_out = jnp.where(frame_keep[None, :], pre_out + input_conv_bias[:, None], 0.0).astype(
        jnp.bfloat16
    )
    phases = jnp.dot(transposed_conv_weight, pre_out, preferred_element_type=jnp.float32).reshape(
        KT, channels, most_rows
    )
    pad_up = UP // 2
    direct = phases[pad_up : pad_up + UP]
    early_part = shifted(phases[UP + pad_up :], -1)
    late_part = shifted(phases[: UP - pad_up], 1)
    phase_sum = direct + jnp.concatenate([early_part, late_part], axis=0)
    woven_out = (
        jnp.transpose(phase_sum, (1, 2, 0)).reshape(channels, most_rows * UP)
        + transposed_conv_bias[:, None]
    )
    sample_keep_mask = jnp.arange(most_rows * UP) < utterance_frames_length * UP
    upsampled = jnp.where(sample_keep_mask[None, :], woven_out, 0.0).astype(jnp.bfloat16)
    first_snake_output = snake(upsampled.astype(jnp.float32), snake_freq_first).astype(jnp.bfloat16)
    inner_convolved = dilated_output(
        first_snake_output, dilated_conv_weight, dilated_conv_bias, DILATION_RATE, sample_keep_mask
    )
    second_act = snake(inner_convolved, snake_freq_second).astype(jnp.bfloat16)
    outer_conv = dilated_output(
        second_act, second_conv_weight, second_conv_bias, 1, sample_keep_mask
    )
    return (upsampled.astype(jnp.float32) + outer_conv).astype(jnp.bfloat16)


def local(
    hidden,
    noisy_mel_state,
    modulation,
    feedforward_in_weight,
    feedforward_in_bias,
    feedforward_out_weight,
    feedforward_out_bias,
    mel_velocity_weight,
    mel_velocity_bias,
    input_conv_weight,
    input_conv_bias,
    transposed_conv_weight,
    transposed_conv_bias,
    snake_freq_first,
    dilated_conv_weight,
    dilated_conv_bias,
    snake_freq_second,
    second_conv_weight,
    second_conv_bias,
    frame_holder,
    frame_position,
    holder_utterance_length,
):
    step_size = math.cos(0.5 * math.pi * (NFE - 1) / NFE)
    cores = lax.axis_size("branch")
    chips = lax.axis_size("seq")
    owners = cores * chips
    own_velocity = velocity(
        hidden[0],
        modulation,
        feedforward_in_weight,
        feedforward_in_bias,
        feedforward_out_weight,
        feedforward_out_bias,
        jnp.pad(mel_velocity_weight, ((0, 0), (0, LANES - mel_velocity_weight.shape[1]))),
        jnp.pad(mel_velocity_bias, (0, LANES - mel_velocity_bias.shape[0])),
    )
    mel_bins = mel_velocity_weight.shape[1]
    frame_count = own_velocity.shape[0]
    half_rows = frame_count // cores
    group = half_rows // chips
    branch_side = lax.axis_index("branch")
    own_half = lax.dynamic_slice_in_dim(own_velocity, branch_side * half_rows, half_rows, 0)
    sent_half = lax.dynamic_slice_in_dim(own_velocity, (1 - branch_side) * half_rows, half_rows, 0)
    peer_half = lax.ppermute(sent_half, "branch", [(0, 1), (1, 0)])
    conditional = jnp.where(branch_side == 0, own_half, peer_half)
    unconditional = jnp.where(branch_side == 0, peer_half, own_half)
    guided = (1.0 + GUIDE) * conditional - GUIDE * unconditional
    noisy_half = lax.dynamic_slice_in_dim(noisy_mel_state, branch_side * half_rows, half_rows, 1)
    noisy_rows = jnp.pad(noisy_half.T, ((0, 0), (0, LANES - mel_bins)))
    refined = noisy_rows + step_size * guided
    owner_half = lax.dynamic_slice_in_dim(frame_holder, branch_side * half_rows, half_rows, 0)
    offset_half = lax.dynamic_slice_in_dim(frame_position, branch_side * half_rows, half_rows, 0)
    lane = jnp.arange(LANES)[None, :]
    refined = jnp.where(lane == mel_bins, owner_half[:, None].astype(jnp.float32), refined)
    first_flag = (offset_half == 0).astype(jnp.float32)[:, None]
    refined = jnp.where(lane == mel_bins + 1, first_flag, refined)
    packed = refined.astype(jnp.bfloat16).reshape(chips, group, LANES)
    spread = lax.all_to_all(packed, "seq", 0, 0, tiled=True)
    rows = spread.reshape(chips * group, LANES)
    owner_of = rows[:, mel_bins].astype(jnp.int32)
    slot_of = owner_of * group + jnp.arange(chips * group, dtype=jnp.int32) % group
    onehot = (slot_of[:, None] == jnp.arange(owners * group, dtype=jnp.int32)[None, :]).astype(
        jnp.bfloat16
    )
    slots = lax.dot_general(
        onehot, rows, (((0,), (0,)), ((), ())), preferred_element_type=jnp.float32
    ).astype(jnp.bfloat16)
    arrived = lax.all_to_all(
        slots.reshape(owners, group, LANES), ("branch", "seq"), 0, 0, tiled=True
    ).reshape(owners * group, LANES)
    start = jnp.sum(
        jnp.arange(owners * group, dtype=jnp.float32) * arrived[:, mel_bins + 1].astype(jnp.float32)
    ).astype(jnp.int32)
    twice = jnp.concatenate([arrived, arrived], axis=0)
    holder_mel = lax.dynamic_slice_in_dim(twice, start, owners * group, 0)[:, :mel_bins].T
    self_owner = lax.axis_index(("branch", "seq"))
    utterance_frames_length = holder_utterance_length[self_owner]
    wave = vocoder_synthesize(
        holder_mel,
        utterance_frames_length,
        input_conv_weight,
        input_conv_bias,
        transposed_conv_weight,
        transposed_conv_bias,
        snake_freq_first,
        dilated_conv_weight,
        dilated_conv_bias,
        snake_freq_second,
        second_conv_weight,
        second_conv_bias,
    )
    return wave[None]


def solution(mesh):
    return jax.shard_map(
        local,
        mesh=mesh,
        in_specs=(
            P("branch", "seq", None),
            P(None, "seq"),
            P(),
            P(),
            P(),
            P(),
            P(),
            P(),
            P(),
            P(),
            P(),
            P(),
            P(),
            P(),
            P(),
            P(),
            P(),
            P(),
            P(),
            P("seq"),
            P("seq"),
            P(),
        ),
        out_specs=P(("branch", "seq"), None, None),
        check_vma=False,
    )
```

```python
import functools
import math

import jax
import jax.numpy as jnp
from jax import lax
from jax.experimental import pallas as pl
from jax.experimental.pallas import tpu as pltpu
from jax.sharding import PartitionSpec as P

UP = 8
KT = 16
KPRE = 7
DILATION_RATE = 3
NFE = 16


GUIDE = 2.0
LANES = 128


def layer_norm(row_block):
    row_mean = jnp.mean(row_block, axis=-1, keepdims=True)
    centred = row_block - row_mean
    row_var = jnp.mean(centred * centred, axis=-1, keepdims=True)
    return centred * lax.rsqrt(row_var + 1e-06)


def velocity(
    row_block,
    modulation,
    feedforward_in_weight,
    feedforward_in_bias,
    feedforward_out_weight,
    feedforward_out_bias,
    mel_velocity_weight,
    mel_velocity_bias,
):
    residual_in = row_block.astype(jnp.float32)
    normed = (layer_norm(residual_in) * (1.0 + modulation[1]) + modulation[0]).astype(jnp.bfloat16)
    inner_pre = (
        jnp.dot(normed, feedforward_in_weight, preferred_element_type=jnp.float32)
        + feedforward_in_bias
    )
    active = jax.nn.gelu(inner_pre, approximate=True).astype(jnp.bfloat16)
    back_proj = (
        jnp.dot(active, feedforward_out_weight, preferred_element_type=jnp.float32)
        + feedforward_out_bias
    )
    block_out = residual_in + modulation[2] * back_proj
    final_norm = (layer_norm(block_out) * (1.0 + modulation[4]) + modulation[3]).astype(
        jnp.bfloat16
    )
    speed = jnp.dot(final_norm, mel_velocity_weight, preferred_element_type=jnp.float32)
    return speed + mel_velocity_bias


SIN_TERMS = (
    3.141592579805583,
    -5.167706866168128,
    2.550031193522954,
    -0.5980441939334223,
    0.07721838619602994,
)


def snake_rows(signal, turns, inverse):
    half_turns = signal * turns
    part = half_turns - jnp.round(half_turns)
    square = part * part
    poly = SIN_TERMS[4] * square + SIN_TERMS[3]
    poly = poly * square + SIN_TERMS[2]
    poly = poly * square + SIN_TERMS[1]
    poly = poly * square + SIN_TERMS[0]
    sine = poly * part
    return signal + sine * sine * inverse


def nt_dot(left, right):
    return lax.dot_general(
        left, right, (((1,), (1,)), ((), ())), preferred_element_type=jnp.float32
    )


def vocoder_kernel(
    length_ref,
    arrived_ref,
    input_weight_ref,
    input_bias_ref,
    up_weight_ref,
    up_bias_ref,
    freq_first_ref,
    dilated_weight_ref,
    dilated_bias_ref,
    freq_second_ref,
    second_weight_ref,
    second_bias_ref,
    wave_ref,
    mel_ref,
    taps_ref,
    shift_wide_ref,
    pre_ref,
    shift_ref,
    up_ref,
    first_ref,
    second_ref,
    out_ref,
    *,
    mel_bins,
):
    frames = arrived_ref.shape[0]
    channels = second_bias_ref.shape[1]
    block = 128
    blocks = frames // block
    halo = 8
    f32, bf16 = jnp.float32, jnp.bfloat16
    step = pl.program_id(0)
    length = length_ref[0]

    def keep_rows(first, count):
        row = lax.broadcasted_iota(jnp.int32, (count, 1), 0) + first
        return row < length

    @pl.when(step == 0)
    def _():
        arrived = arrived_ref[...]
        lane = lax.broadcasted_iota(jnp.int32, arrived.shape, 1)
        place = lax.broadcasted_iota(jnp.int32, arrived.shape, 0).astype(f32)
        start = jnp.sum(
            jnp.where(lane == mel_bins + 1, arrived.astype(f32) * place, 0.0), keepdims=True
        ).astype(jnp.int32)
        mel_ref[...] = jnp.zeros(mel_ref.shape, f32)
        for i in range(blocks):
            ahead = (
                lax.broadcasted_iota(jnp.int32, (block, frames), 1)
                - lax.broadcasted_iota(jnp.int32, (block, frames), 0)
                - (start + i * block)
            )
            pick = ((ahead == 0) | (ahead == -frames)).astype(bf16)
            mel_ref[halo + i * block : halo + (i + 1) * block, :] = jnp.dot(
                pick, arrived, preferred_element_type=f32
            )
        for k in range(KPRE):
            low = halo + k - KPRE // 2
            taps_ref[:, k * LANES : (k + 1) * LANES] = mel_ref[low : low + frames, :].astype(bf16)
        shift_wide_ref[...] = jnp.zeros(shift_wide_ref.shape, f32)
        for i in range(blocks):
            rows = slice(i * block, (i + 1) * block)
            pre = jnp.dot(taps_ref[rows, :], input_weight_ref[...], preferred_element_type=f32)
            pre = jnp.where(keep_rows(i * block, block), pre + input_bias_ref[...], 0.0)
            shift_wide_ref[halo + i * block : halo + (i + 1) * block, :] = pre
        for k in range(3):
            low = halo + k - 1
            pre_ref[k] = shift_wide_ref[low : low + frames, :].astype(bf16)
        shift_ref[...] = jnp.zeros(shift_ref.shape, f32)

        turns_first = freq_first_ref[...] * (1.0 / math.pi)
        inverse_first = 1.0 / freq_first_ref[...]
        turns_second = freq_second_ref[...] * (1.0 / math.pi)
        inverse_second = 1.0 / freq_second_ref[...]

        def neighbour_rows(offset):
            low = halo + offset
            return shift_ref[low : low + frames, :].astype(bf16)

        @pl.loop(0, UP)
        def _(r):
            side = jnp.where(r < UP // 2, 0, 2)
            here = up_weight_ref[r + UP // 2]
            there = up_weight_ref[lax.rem(r + UP // 2 + UP, KT)]
            for i in range(blocks):
                rows = slice(i * block, (i + 1) * block)
                up = nt_dot(pre_ref[1, rows, :], here) + nt_dot(pre_ref[side, rows, :], there)
                up = jnp.where(keep_rows(i * block, block), up + up_bias_ref[...], 0.0)
                up = up.astype(bf16)
                up_ref[r, rows, :] = up
                first = snake_rows(up.astype(f32), turns_first, inverse_first)
                first_ref[r + 3, rows, :] = first.astype(bf16)

        for r in range(DILATION_RATE):
            shift_ref[halo : halo + frames, :] = first_ref[r + 3].astype(f32)
            first_ref[r + 3 + UP] = neighbour_rows(1)
        for r in range(UP - DILATION_RATE, UP):
            shift_ref[halo : halo + frames, :] = first_ref[r + 3].astype(f32)
            first_ref[r + 3 - UP] = neighbour_rows(-1)

        @pl.loop(0, UP)
        def _(r):
            for i in range(blocks):
                rows = slice(i * block, (i + 1) * block)
                inner = jnp.dot(
                    first_ref[r, rows, :], dilated_weight_ref[0], preferred_element_type=f32
                )
                inner += jnp.dot(
                    first_ref[r + 3, rows, :], dilated_weight_ref[1], preferred_element_type=f32
                )
                inner += jnp.dot(
                    first_ref[r + 6, rows, :], dilated_weight_ref[2], preferred_element_type=f32
                )
                inner = jnp.where(
                    keep_rows(i * block, block), inner + dilated_bias_ref[...], 0.0
                )
                second = snake_rows(inner, turns_second, inverse_second)
                second_ref[r + 1, rows, :] = second.astype(bf16)

        shift_ref[halo : halo + frames, :] = second_ref[1].astype(f32)
        second_ref[UP + 1] = neighbour_rows(1)
        shift_ref[halo : halo + frames, :] = second_ref[UP].astype(f32)
        second_ref[0] = neighbour_rows(-1)

    base = pl.multiple_of(step * block, block)
    for r in range(UP):
        rows = pl.ds(base, block)
        outer = jnp.dot(second_ref[r, rows, :], second_weight_ref[0], preferred_element_type=f32)
        outer += jnp.dot(
            second_ref[r + 1, rows, :], second_weight_ref[1], preferred_element_type=f32
        )
        outer += jnp.dot(
            second_ref[r + 2, rows, :], second_weight_ref[2], preferred_element_type=f32
        )
        outer = jnp.where(keep_rows(base, block), outer + second_bias_ref[...], 0.0)
        out_ref[r] = (up_ref[r, rows, :].astype(f32) + outer).astype(bf16)
    narrow = 256 // UP
    row = lax.broadcasted_iota(jnp.int32, (256, 256), 0)
    col = lax.broadcasted_iota(jnp.int32, (256, 256), 1)
    weave = (col == lax.rem(row, narrow) * UP + row // narrow).astype(bf16)
    for piece in range(block // narrow):
        phases = jnp.concatenate(
            [out_ref[r, piece * narrow : (piece + 1) * narrow, :] for r in range(UP)], axis=0
        )
        woven = lax.dot_general(
            phases, weave, (((0,), (0,)), ((), ())), preferred_element_type=f32
        )
        wave_ref[0, :, piece * 256 : (piece + 1) * 256] = woven.astype(bf16)


def vocoder(
    arrived,
    length,
    mel_bins,
    input_conv_weight,
    input_conv_bias,
    transposed_conv_weight,
    transposed_conv_bias,
    snake_freq_first,
    dilated_conv_weight,
    dilated_conv_bias,
    snake_freq_second,
    second_conv_weight,
    second_conv_bias,
):
    frames = arrived.shape[0]
    wide = input_conv_bias.shape[0]
    channels = transposed_conv_bias.shape[0]
    block = 128
    f32, bf16 = jnp.float32, jnp.bfloat16
    taps_weight = jnp.pad(
        input_conv_weight.reshape(KPRE, mel_bins, wide), ((0, 0), (0, LANES - mel_bins), (0, 0))
    ).reshape(KPRE * LANES, wide)
    operands = [
        arrived,
        taps_weight,
        input_conv_bias[None],
        transposed_conv_weight.reshape(KT, channels, wide),
        transposed_conv_bias[None],
        snake_freq_first[None],
        dilated_conv_weight.reshape(3, channels, channels),
        dilated_conv_bias[None],
        snake_freq_second[None],
        second_conv_weight.reshape(3, channels, channels),
        second_conv_bias[None],
    ]
    return pl.pallas_call(
        functools.partial(vocoder_kernel, mel_bins=mel_bins),
        out_shape=jax.ShapeDtypeStruct((1, channels, frames * UP), bf16),
        grid=(frames // block,),
        in_specs=[pl.BlockSpec(memory_space=pltpu.SMEM)]
        + [
            pl.BlockSpec(
                x.shape, lambda i, n=x.ndim: (0,) * n, pipeline_mode=pl.Buffered(1)
            )
            for x in operands
        ],
        out_specs=pl.BlockSpec((1, channels, block * UP), lambda i: (0, 0, i)),
        scratch_shapes=[
            pltpu.VMEM((frames + 16, LANES), f32),
            pltpu.VMEM((frames, KPRE * LANES), bf16),
            pltpu.VMEM((frames + 16, wide), f32),
            pltpu.VMEM((3, frames, wide), bf16),
            pltpu.VMEM((frames + 16, channels), f32),
            pltpu.VMEM((UP, frames, channels), bf16),
            pltpu.VMEM((UP + 6, frames, channels), bf16),
            pltpu.VMEM((UP + 2, frames, channels), bf16),
            pltpu.VMEM((UP, block, channels), bf16),
        ],
        compiler_params=pltpu.CompilerParams(vmem_limit_bytes=48 * 1024 * 1024),
        name="vocoder",
    )(length, *operands)


def local(
    hidden,
    noisy_mel_state,
    modulation,
    feedforward_in_weight,
    feedforward_in_bias,
    feedforward_out_weight,
    feedforward_out_bias,
    mel_velocity_weight,
    mel_velocity_bias,
    input_conv_weight,
    input_conv_bias,
    transposed_conv_weight,
    transposed_conv_bias,
    snake_freq_first,
    dilated_conv_weight,
    dilated_conv_bias,
    snake_freq_second,
    second_conv_weight,
    second_conv_bias,
    frame_holder,
    frame_position,
    holder_utterance_length,
):
    step_size = math.cos(0.5 * math.pi * (NFE - 1) / NFE)
    cores = lax.axis_size("branch")
    chips = lax.axis_size("seq")
    owners = cores * chips
    own_velocity = velocity(
        hidden[0],
        modulation,
        feedforward_in_weight,
        feedforward_in_bias,
        feedforward_out_weight,
        feedforward_out_bias,
        jnp.pad(mel_velocity_weight, ((0, 0), (0, LANES - mel_velocity_weight.shape[1]))),
        jnp.pad(mel_velocity_bias, (0, LANES - mel_velocity_bias.shape[0])),
    )
    mel_bins = mel_velocity_weight.shape[1]
    frame_count = own_velocity.shape[0]
    half_rows = frame_count // cores
    group = half_rows // chips
    branch_side = lax.axis_index("branch")
    own_half = lax.dynamic_slice_in_dim(own_velocity, branch_side * half_rows, half_rows, 0)
    sent_half = lax.dynamic_slice_in_dim(own_velocity, (1 - branch_side) * half_rows, half_rows, 0)
    peer_half = lax.ppermute(sent_half, "branch", [(0, 1), (1, 0)])
    conditional = jnp.where(branch_side == 0, own_half, peer_half)
    unconditional = jnp.where(branch_side == 0, peer_half, own_half)
    guided = (1.0 + GUIDE) * conditional - GUIDE * unconditional
    noisy_half = lax.dynamic_slice_in_dim(noisy_mel_state, branch_side * half_rows, half_rows, 1)
    noisy_rows = jnp.pad(noisy_half.T, ((0, 0), (0, LANES - mel_bins)))
    refined = noisy_rows + step_size * guided
    owner_half = lax.dynamic_slice_in_dim(frame_holder, branch_side * half_rows, half_rows, 0)
    offset_half = lax.dynamic_slice_in_dim(frame_position, branch_side * half_rows, half_rows, 0)
    lane = jnp.arange(LANES)[None, :]
    refined = jnp.where(lane == mel_bins, owner_half[:, None].astype(jnp.float32), refined)
    first_flag = (offset_half == 0).astype(jnp.float32)[:, None]
    refined = jnp.where(lane == mel_bins + 1, first_flag, refined)
    packed = refined.astype(jnp.bfloat16).reshape(chips, group, LANES)
    spread = lax.all_to_all(packed, "seq", 0, 0, tiled=True)
    rows = spread.reshape(chips * group, LANES)
    owner_of = rows[:, mel_bins].astype(jnp.int32)
    slot_of = owner_of * group + jnp.arange(chips * group, dtype=jnp.int32) % group
    onehot = (slot_of[:, None] == jnp.arange(owners * group, dtype=jnp.int32)[None, :]).astype(
        jnp.bfloat16
    )
    slots = lax.dot_general(
        onehot, rows, (((0,), (0,)), ((), ())), preferred_element_type=jnp.float32
    ).astype(jnp.bfloat16)
    arrived = lax.all_to_all(
        slots.reshape(owners, group, LANES), ("branch", "seq"), 0, 0, tiled=True
    ).reshape(owners * group, LANES)
    self_owner = lax.axis_index(("branch", "seq"))
    length = lax.dynamic_slice_in_dim(holder_utterance_length, self_owner, 1, 0)
    return vocoder(
        arrived,
        length,
        mel_bins,
        input_conv_weight,
        input_conv_bias,
        transposed_conv_weight,
        transposed_conv_bias,
        snake_freq_first,
        dilated_conv_weight,
        dilated_conv_bias,
        snake_freq_second,
        second_conv_weight,
        second_conv_bias,
    )


def solution(mesh):
    return jax.shard_map(
        local,
        mesh=mesh,
        in_specs=(
            P("branch", "seq", None),
            P(None, "seq"),
            P(),
            P(),
            P(),
            P(),
            P(),
            P(),
            P(),
            P(),
            P(),
            P(),
            P(),
            P(),
            P(),
            P(),
            P(),
            P(),
            P(),
            P("seq"),
            P("seq"),
            P(),
        ),
        out_specs=P(("branch", "seq"), None, None),
        check_vma=False,
    )
```

```python
import functools
import math

import jax
import jax.numpy as jnp
from jax import lax
from jax.experimental import pallas as pl
from jax.experimental.pallas import tpu as pltpu
from jax.sharding import PartitionSpec as P

UP = 8
KT = 16
KPRE = 7
DILATION_RATE = 3
NFE = 16


GUIDE = 2.0
LANES = 128
GROUP = 8
GELU_SCALE = math.sqrt(2.0 / math.pi)


def layer_norm(row_block):
    row_mean = jnp.mean(row_block, axis=-1, keepdims=True)
    centred = row_block - row_mean
    row_var = jnp.mean(centred * centred, axis=-1, keepdims=True)
    return centred * lax.rsqrt(row_var + 1e-06)


def gelu_tanh(inner):
    slope = inner * (GELU_SCALE + (GELU_SCALE * 0.044715) * (inner * inner))
    half = 0.5 * inner
    return half + half * jnp.tanh(slope)


def velocity_kernel(
    side_ref,
    hidden_ref,
    modulation_ref,
    in_weight_ref,
    in_bias_ref,
    out_weight_ref,
    out_bias_ref,
    mel_weight_ref,
    mel_bias_ref,
    noisy_ref,
    holder_ref,
    position_ref,
    own_ref,
    sent_ref,
    base_ref,
    tall_ref,
    normed_ref,
    total_ref,
    *,
    block,
):
    frames = hidden_ref.shape[1]
    half_rows = own_ref.shape[0]
    norm_block = 128
    f32, bf16 = jnp.float32, jnp.bfloat16
    step = pl.program_id(0)

    @pl.when(step == 0)
    def _():
        scale = 1.0 + modulation_ref[1:2, :]
        for low in range(0, frames, norm_block):
            rows = slice(low, low + norm_block)
            normed = layer_norm(hidden_ref[0, rows, :].astype(f32)) * scale + modulation_ref[0:1, :]
            normed_ref[rows, :] = normed.astype(bf16)
            total_ref[rows, :] = jnp.broadcast_to(
                out_bias_ref[...], (norm_block, out_bias_ref.shape[1])
            )

        mel_bins = noisy_ref.shape[0]
        half = pl.ds(pl.multiple_of(side_ref[0] * half_rows, half_rows), half_rows)
        tall_ref[...] = jnp.zeros(tall_ref.shape, f32)
        tall_ref[:mel_bins, :] = noisy_ref[:, half]
        tall_ref[mel_bins : mel_bins + 1, :] = holder_ref[:, half].astype(f32)
        first_flag = jnp.where(position_ref[:, half] == 0, 1.0, 0.0)
        tall_ref[mel_bins + 1 : mel_bins + 2, :] = first_flag
        base_ref[...] = tall_ref[...].T

    for low in range(0, frames, block):
        rows = slice(low, low + block)
        inner = jnp.dot(normed_ref[rows, :], in_weight_ref[...], preferred_element_type=f32)
        active = gelu_tanh(inner + in_bias_ref[...]).astype(bf16)
        total_ref[rows, :] += jnp.dot(active, out_weight_ref[...], preferred_element_type=f32)

    @pl.when(step == pl.num_programs(0) - 1)
    def _():
        scale = 1.0 + modulation_ref[4:5, :]
        for low in range(0, frames, norm_block):
            rows = slice(low, low + norm_block)
            block_out = hidden_ref[0, rows, :].astype(f32) + modulation_ref[2:3, :] * total_ref[rows, :]
            normed_ref[rows, :] = (
                layer_norm(block_out) * scale + modulation_ref[3:4, :]
            ).astype(bf16)
        for part in range(2):
            rows = slice(part * half_rows, (part + 1) * half_rows)
            speed = (
                jnp.dot(normed_ref[rows, :], mel_weight_ref[...], preferred_element_type=f32)
                + mel_bias_ref[...]
            )

            @pl.when(side_ref[0] == part)
            def _(speed=speed):
                own_ref[...] = speed

            @pl.when(side_ref[0] != part)
            def _(speed=speed):
                sent_ref[...] = speed


def velocity_halves(
    side,
    hidden,
    modulation,
    feedforward_in_weight,
    feedforward_in_bias,
    feedforward_out_weight,
    feedforward_out_bias,
    mel_velocity_weight,
    mel_velocity_bias,
    noisy_mel_state,
    frame_holder,
    frame_position,
    block=768,
    chunk=1024,
):
    frames, width = hidden.shape[1:]
    hidden_units = feedforward_in_weight.shape[1]
    mel_bins = mel_velocity_weight.shape[1]
    half = jax.ShapeDtypeStruct((frames // 2, LANES), jnp.float32)
    whole = pl.Buffered(1)
    fixed = lambda i: (0, 0)
    return pl.pallas_call(
        functools.partial(velocity_kernel, block=block),
        out_shape=(half, half, half),
        grid=(hidden_units // chunk,),
        in_specs=[
            pl.BlockSpec(memory_space=pltpu.SMEM),
            pl.BlockSpec((1, frames, width), lambda i: (0, 0, 0), pipeline_mode=whole),
            pl.BlockSpec(modulation.shape, fixed, pipeline_mode=whole),
            pl.BlockSpec((width, chunk), lambda i: (0, i)),
            pl.BlockSpec((1, chunk), lambda i: (0, i)),
            pl.BlockSpec((chunk, width), lambda i: (i, 0)),
            pl.BlockSpec((1, width), fixed, pipeline_mode=whole),
            pl.BlockSpec((width, LANES), fixed, pipeline_mode=whole),
            pl.BlockSpec((1, LANES), fixed, pipeline_mode=whole),
            pl.BlockSpec(noisy_mel_state.shape, fixed, pipeline_mode=whole),
            pl.BlockSpec((1, frames), fixed, pipeline_mode=whole),
            pl.BlockSpec((1, frames), fixed, pipeline_mode=whole),
        ],
        out_specs=(pl.BlockSpec(half.shape, fixed),) * 3,
        scratch_shapes=[
            pltpu.VMEM((LANES, frames // 2), jnp.float32),
            pltpu.VMEM((frames, width), jnp.bfloat16),
            pltpu.VMEM((frames, width), jnp.float32),
        ],
        compiler_params=pltpu.CompilerParams(vmem_limit_bytes=40 * 1024 * 1024),
        name="velocity",
    )(
        side,
        hidden,
        modulation,
        feedforward_in_weight,
        feedforward_in_bias[None],
        feedforward_out_weight,
        feedforward_out_bias[None],
        jnp.pad(mel_velocity_weight, ((0, 0), (0, LANES - mel_bins))),
        jnp.pad(mel_velocity_bias, (0, LANES - mel_bins))[None],
        noisy_mel_state,
        frame_holder[None],
        frame_position[None],
    )


def combine_kernel(side_ref, own_ref, peer_ref, base_ref, packed_ref, spaced_ref):
    chips = packed_ref.shape[0]
    step_size = math.cos(0.5 * math.pi * (NFE - 1) / NFE)
    first = side_ref[0] == 0
    conditional = jnp.where(first, own_ref[...], peer_ref[...])
    unconditional = jnp.where(first, peer_ref[...], own_ref[...])
    guided = (1.0 + GUIDE) * conditional - GUIDE * unconditional
    refined = base_ref[...] + step_size * guided
    for turn in range(GROUP):
        low = turn * chips
        if low < refined.shape[0]:
            spaced_ref[pl.ds(turn, chips, stride=GROUP), :] = refined[low : low + chips, :]
        else:
            spaced_ref[pl.ds(turn, chips, stride=GROUP), :] = jnp.zeros((chips, LANES), jnp.float32)
    packed_ref[...] = spaced_ref[...].reshape(packed_ref.shape).astype(packed_ref.dtype)


def sort_kernel(spread_ref, slots_ref, spaced_ref, *, mel_bins):
    owners = slots_ref.shape[0]
    rows = spread_ref[...].reshape(-1, LANES)
    count = rows.shape[0]
    column = jnp.broadcast_to(rows[:, mel_bins : mel_bins + 1].astype(jnp.float32), (count, owners))
    owner_of = column.T
    owner = lax.broadcasted_iota(jnp.int32, (owners, count), 0).astype(jnp.float32)
    turn_of = lax.rem(lax.broadcasted_iota(jnp.int32, (1, count), 1), GROUP)
    for turn in range(GROUP):
        pick = ((owner_of == owner) & (turn_of == turn)).astype(jnp.bfloat16)
        spaced_ref[pl.ds(turn, owners, stride=GROUP), :] = jnp.dot(
            pick, rows, preferred_element_type=jnp.float32
        )
    slots_ref[...] = spaced_ref[...].reshape(slots_ref.shape).astype(slots_ref.dtype)


SIN_TERMS = (
    3.141592579805583,
    -5.167706866168128,
    2.550031193522954,
    -0.5980441939334223,
    0.07721838619602994,
)


def snake_rows(signal, turns, inverse):
    half_turns = signal * turns
    part = half_turns - jnp.round(half_turns)
    square = part * part
    poly = SIN_TERMS[4] * square + SIN_TERMS[3]
    poly = poly * square + SIN_TERMS[2]
    poly = poly * square + SIN_TERMS[1]
    poly = poly * square + SIN_TERMS[0]
    sine = poly * part
    return signal + sine * sine * inverse


def nt_dot(left, right):
    return lax.dot_general(
        left, right, (((1,), (1,)), ((), ())), preferred_element_type=jnp.float32
    )


def vocoder_kernel(
    length_ref,
    arrived_ref,
    input_weight_ref,
    input_bias_ref,
    up_weight_hbm,
    up_bias_ref,
    freq_first_ref,
    dilated_weight_ref,
    dilated_bias_ref,
    freq_second_ref,
    second_weight_ref,
    second_bias_ref,
    wave_ref,
    mel_ref,
    taps_ref,
    shift_wide_ref,
    pre_ref,
    shift_ref,
    up_ref,
    first_ref,
    second_ref,
    out_ref,
    up_weight_ref,
    up_sem,
    even_ref,
    odd_ref,
    *,
    mel_bins,
    block,
):
    frames = up_ref.shape[1]
    piece_frames = out_ref.shape[1] // pl.num_programs(0)
    part_rows = arrived_ref.shape[0] // 2
    blocks = frames // block
    halo = 8
    f32, bf16 = jnp.float32, jnp.bfloat16
    step = pl.program_id(0)
    length = length_ref[0]

    def keep_rows(first, count):
        row = lax.broadcasted_iota(jnp.int32, (count, 1), 0) + first
        return row < length

    @pl.when(step == 0)
    def _():
        up_copy = pltpu.make_async_copy(up_weight_hbm, up_weight_ref, up_sem)
        up_copy.start()
        arrived = arrived_ref[...]

        def shard_row(shape, axis):
            i = lax.broadcasted_iota(jnp.int32, shape, axis)
            side = (i >= part_rows).astype(jnp.int32)
            inner = i - side * part_rows
            turn = lax.rem(inner, GROUP)
            row = side * (frames // 2) + turn * (part_rows // GROUP) + inner // GROUP
            return jnp.where(turn < frames * GROUP // (2 * part_rows), row, -4 * frames)

        lane = lax.broadcasted_iota(jnp.int32, arrived.shape, 1)
        flagged = jnp.where(lane == mel_bins + 1, arrived.astype(f32), 0.0)
        start = jnp.sum(
            jnp.where(flagged > 0.5, shard_row(arrived.shape, 0).astype(f32), 0.0), keepdims=True
        ).astype(jnp.int32)
        mel_ref[...] = jnp.zeros(mel_ref.shape, f32)
        turned = shard_row((1, arrived.shape[0]), 1) - start
        for i in range(frames // 128):
            ahead = turned - i * 128 - lax.broadcasted_iota(jnp.int32, (128, 1), 0)
            pick = ((ahead == 0) | (ahead == -frames)).astype(bf16)
            mel_ref[halo + i * 128 : halo + (i + 1) * 128, :] = jnp.dot(
                pick, arrived, preferred_element_type=f32
            )
        for k in range(KPRE):
            low = halo + k - KPRE // 2
            taps_ref[:, k * LANES : (k + 1) * LANES] = mel_ref[low : low + frames, :].astype(bf16)
        shift_wide_ref[...] = jnp.zeros(shift_wide_ref.shape, f32)
        for i in range(blocks):
            rows = slice(i * block, (i + 1) * block)
            pre = jnp.dot(taps_ref[rows, :], input_weight_ref[...], preferred_element_type=f32)
            pre = jnp.where(keep_rows(i * block, block), pre + input_bias_ref[...], 0.0)
            shift_wide_ref[halo + i * block : halo + (i + 1) * block, :] = pre
        for k in range(3):
            low = halo + k - 1
            pre_ref[k] = shift_wide_ref[low : low + frames, :].astype(bf16)
        shift_ref[...] = jnp.zeros(shift_ref.shape, f32)

        turns_first = freq_first_ref[...] * (1.0 / math.pi)
        inverse_first = 1.0 / freq_first_ref[...]
        turns_second = freq_second_ref[...] * (1.0 / math.pi)
        inverse_second = 1.0 / freq_second_ref[...]

        def neighbour_rows(offset):
            low = halo + offset
            return shift_ref[low : low + frames, :].astype(bf16)

        up_copy.wait()

        def pipeline(product, finish):
            for i in range(blocks):
                rows = slice(i * block, (i + 1) * block)
                even_ref[rows, :] = product(0, rows)

            @pl.loop(0, UP // 2)
            def _(pair):
                for r, ready_ref, r_next, next_ref in (
                    (2 * pair, even_ref, 2 * pair + 1, odd_ref),
                    (2 * pair + 1, odd_ref, jnp.minimum(2 * pair + 2, UP - 1), even_ref),
                ):
                    for i in range(blocks):
                        rows = slice(i * block, (i + 1) * block)
                        next_ref[rows, :] = product(r_next, rows)
                        for low in range(i * block, (i + 1) * block, 64):
                            finish(r, low, ready_ref[low : low + 64, :])

        def up_product(r, rows):
            side = jnp.where(r < UP // 2, 0, 2)
            return jnp.dot(
                jnp.concatenate([pre_ref[1, rows, :], pre_ref[side, rows, :]], axis=1),
                jnp.concatenate(
                    [up_weight_ref[r + UP // 2], up_weight_ref[lax.rem(r + UP // 2 + UP, KT)]],
                    axis=0,
                ),
                preferred_element_type=f32,
            )

        def up_finish(r, low, up):
            rows = slice(low, low + 64)
            up = jnp.where(keep_rows(low, 64), up + up_bias_ref[...], 0.0)
            up = up.astype(bf16)
            up_ref[r, rows, :] = up
            first = snake_rows(up.astype(f32), turns_first, inverse_first)
            first_ref[r + 3, rows, :] = first.astype(bf16)

        pipeline(up_product, up_finish)

        for r in range(DILATION_RATE):
            shift_ref[halo : halo + frames, :] = first_ref[r + 3].astype(f32)
            first_ref[r + 3 + UP] = neighbour_rows(1)
        for r in range(UP - DILATION_RATE, UP):
            shift_ref[halo : halo + frames, :] = first_ref[r + 3].astype(f32)
            first_ref[r + 3 - UP] = neighbour_rows(-1)

        def inner_product(r, rows):
            around = [first_ref[r + DILATION_RATE * k, rows, :] for k in range(3)]
            return jnp.dot(
                jnp.concatenate(around, axis=1),
                dilated_weight_ref[...],
                preferred_element_type=f32,
            )

        def inner_finish(r, low, inner):
            inner = jnp.where(keep_rows(low, 64), inner + dilated_bias_ref[...], 0.0)
            second = snake_rows(inner, turns_second, inverse_second)
            second_ref[r + 1, low : low + 64, :] = second.astype(bf16)

        pipeline(inner_product, inner_finish)

        shift_ref[halo : halo + frames, :] = second_ref[1].astype(f32)
        second_ref[UP + 1] = neighbour_rows(1)
        shift_ref[halo : halo + frames, :] = second_ref[UP].astype(f32)
        second_ref[0] = neighbour_rows(-1)

        def outer_product(r, rows):
            around = [second_ref[r + k, rows, :] for k in range(3)]
            return jnp.dot(
                jnp.concatenate(around, axis=1),
                second_weight_ref[...],
                preferred_element_type=f32,
            )

        def outer_finish(r, low, outer):
            rows = slice(low, low + 64)
            outer = jnp.where(keep_rows(low, 64), outer + second_bias_ref[...], 0.0)
            out_ref[r, rows, :] = (up_ref[r, rows, :].astype(f32) + outer).astype(bf16)

        pipeline(outer_product, outer_finish)

    base = pl.multiple_of(step * piece_frames, piece_frames)
    narrow = 256 // UP
    row = lax.broadcasted_iota(jnp.int32, (256, 256), 0)
    col = lax.broadcasted_iota(jnp.int32, (256, 256), 1)
    weave = (col == lax.rem(row, narrow) * UP + row // narrow).astype(bf16)
    for piece in range(piece_frames // narrow):
        rows = pl.ds(base + piece * narrow, narrow)
        phases = jnp.concatenate([out_ref[r, rows, :] for r in range(UP)], axis=0)
        woven = lax.dot_general(
            phases, weave, (((0,), (0,)), ((), ())), preferred_element_type=f32
        )
        wave_ref[0, :, piece * 256 : (piece + 1) * 256] = woven.astype(bf16)


def vocoder(
    arrived,
    length,
    mel_bins,
    input_conv_weight,
    input_conv_bias,
    transposed_conv_weight,
    transposed_conv_bias,
    snake_freq_first,
    dilated_conv_weight,
    dilated_conv_bias,
    snake_freq_second,
    second_conv_weight,
    second_conv_bias,
    frames,
    block=256,
    piece=256,
):
    wide = input_conv_bias.shape[0]
    channels = transposed_conv_bias.shape[0]
    f32, bf16 = jnp.float32, jnp.bfloat16
    taps_weight = jnp.pad(
        input_conv_weight.reshape(KPRE, mel_bins, wide), ((0, 0), (0, LANES - mel_bins), (0, 0))
    ).reshape(KPRE * LANES, wide)
    operands = [
        arrived,
        taps_weight,
        input_conv_bias[None],
        transposed_conv_weight.reshape(KT, channels, wide).transpose(0, 2, 1),
        transposed_conv_bias[None],
        snake_freq_first[None],
        dilated_conv_weight,
        dilated_conv_bias[None],
        snake_freq_second[None],
        second_conv_weight,
        second_conv_bias[None],
    ]
    return pl.pallas_call(
        functools.partial(vocoder_kernel, mel_bins=mel_bins, block=block),
        out_shape=jax.ShapeDtypeStruct((1, channels, frames * UP), bf16),
        grid=(frames // piece,),
        in_specs=[pl.BlockSpec(memory_space=pltpu.SMEM)]
        + [
            pl.BlockSpec(memory_space=pl.ANY)
            if x.ndim == 3 and x.shape[0] == KT
            else pl.BlockSpec(x.shape, lambda i, n=x.ndim: (0,) * n, pipeline_mode=pl.Buffered(1))
            for x in operands
        ],
        out_specs=pl.BlockSpec((1, channels, piece * UP), lambda i: (0, 0, i)),
        scratch_shapes=[
            pltpu.VMEM((frames + 16, LANES), f32),
            pltpu.VMEM((frames, KPRE * LANES), bf16),
            pltpu.VMEM((frames + 16, wide), f32),
            pltpu.VMEM((3, frames, wide), bf16),
            pltpu.VMEM((frames + 16, channels), f32),
            pltpu.VMEM((UP, frames, channels), bf16),
            pltpu.VMEM((UP + 6, frames, channels), bf16),
            pltpu.VMEM((UP + 2, frames, channels), bf16),
            pltpu.VMEM((UP, frames, channels), bf16),
            pltpu.VMEM((KT, wide, channels), bf16),
            pltpu.SemaphoreType.DMA(()),
            pltpu.VMEM((frames, channels), f32),
            pltpu.VMEM((frames, channels), f32),
        ],
        compiler_params=pltpu.CompilerParams(vmem_limit_bytes=48 * 1024 * 1024),
        name="vocoder",
    )(length, *operands)


def local(
    hidden,
    noisy_mel_state,
    modulation,
    feedforward_in_weight,
    feedforward_in_bias,
    feedforward_out_weight,
    feedforward_out_bias,
    mel_velocity_weight,
    mel_velocity_bias,
    input_conv_weight,
    input_conv_bias,
    transposed_conv_weight,
    transposed_conv_bias,
    snake_freq_first,
    dilated_conv_weight,
    dilated_conv_bias,
    snake_freq_second,
    second_conv_weight,
    second_conv_bias,
    frame_holder,
    frame_position,
    holder_utterance_length,
):
    chips = lax.axis_size("seq")
    owners = lax.axis_size("branch") * chips
    mel_bins, frames = noisy_mel_state.shape
    side = lax.axis_index("branch").astype(jnp.int32)[None]
    own_half, sent_half, base = velocity_halves(
        side,
        hidden,
        modulation,
        feedforward_in_weight,
        feedforward_in_bias,
        feedforward_out_weight,
        feedforward_out_bias,
        mel_velocity_weight,
        mel_velocity_bias,
        noisy_mel_state,
        frame_holder,
        frame_position,
    )
    peer_half = lax.ppermute(sent_half, "branch", [(0, 1), (1, 0)])
    packed = pl.pallas_call(
        combine_kernel,
        out_shape=jax.ShapeDtypeStruct((chips, GROUP, LANES), jnp.bfloat16),
        in_specs=[pl.BlockSpec(memory_space=pltpu.SMEM)]
        + [pl.BlockSpec(memory_space=pltpu.VMEM)] * 3,
        scratch_shapes=[pltpu.VMEM((chips * GROUP, LANES), jnp.float32)],
        name="combine",
    )(side, own_half, peer_half, base)
    spread = lax.all_to_all(packed, "seq", 0, 0, tiled=True)
    slots = pl.pallas_call(
        functools.partial(sort_kernel, mel_bins=mel_bins),
        out_shape=jax.ShapeDtypeStruct((owners, GROUP, LANES), jnp.bfloat16),
        scratch_shapes=[pltpu.VMEM((owners * GROUP, LANES), jnp.float32)],
        name="sort",
    )(spread)
    arrived = lax.all_to_all(slots, ("branch", "seq"), 0, 0, tiled=True)
    arrived = arrived.reshape(owners * GROUP, LANES)
    self_owner = lax.axis_index(("branch", "seq"))
    length = lax.dynamic_slice_in_dim(holder_utterance_length, self_owner, 1, 0)
    return vocoder(
        arrived,
        length,
        mel_bins,
        input_conv_weight,
        input_conv_bias,
        transposed_conv_weight,
        transposed_conv_bias,
        snake_freq_first,
        dilated_conv_weight,
        dilated_conv_bias,
        snake_freq_second,
        second_conv_weight,
        second_conv_bias,
        frames,
    )


def solution(mesh):
    return jax.shard_map(
        local,
        mesh=mesh,
        in_specs=(
            P("branch", "seq", None),
            P(None, "seq"),
            P(),
            P(),
            P(),
            P(),
            P(),
            P(),
            P(),
            P(),
            P(),
            P(),
            P(),
            P(),
            P(),
            P(),
            P(),
            P(),
            P(),
            P("seq"),
            P("seq"),
            P(),
        ),
        out_specs=P(("branch", "seq"), None, None),
        check_vma=False,
    )
```

```python
import functools
import math

import jax
import jax.numpy as jnp
from jax import lax
from jax.experimental import pallas as pl
from jax.experimental.pallas import tpu as pltpu
from jax.sharding import PartitionSpec as P

UP = 8
KT = 16
KPRE = 7
DILATION_RATE = 3
NFE = 16


GUIDE = 2.0
LANES = 128
GROUP = 8
GELU_SCALE = math.sqrt(2.0 / math.pi)


def layer_norm(row_block):
    row_mean = jnp.mean(row_block, axis=-1, keepdims=True)
    centred = row_block - row_mean
    row_var = jnp.mean(centred * centred, axis=-1, keepdims=True)
    return centred * lax.rsqrt(row_var + 1e-06)


def gelu_tanh(inner):
    slope = inner * (GELU_SCALE + (GELU_SCALE * 0.044715) * (inner * inner))
    half = 0.5 * inner
    return half + half * jnp.tanh(slope)


def nt_dot(left, right):
    return lax.dot_general(
        left, right, (((1,), (1,)), ((), ())), preferred_element_type=jnp.float32
    )


def velocity_kernel(
    side_ref,
    hidden_hbm,
    modulation_ref,
    in_weight_hbm,
    in_bias_ref,
    out_weight_hbm,
    out_bias_ref,
    mel_weight_ref,
    mel_bias_ref,
    noisy_ref,
    holder_ref,
    position_ref,
    own_ref,
    sent_ref,
    base_ref,
    hidden_ref,
    in_weight_ref,
    out_weight_ref,
    mel_pad_ref,
    bias_pad_ref,
    tall_ref,
    normed_ref,
    active_ref,
    speed_ref,
    back_ref,
    hidden_sem,
    in_sem,
    out_sem,
    *,
    block,
    tail,
    in_chunk,
):
    frames, width = hidden_ref.shape
    units = in_weight_ref.shape[1]
    half_rows = frames // 2
    mel_bins = noisy_ref.shape[0]
    chips = own_ref.shape[0] // GROUP
    f32, bf16 = jnp.float32, jnp.bfloat16
    hidden_copies = []
    for i in range(frames // block):
        rows = pl.ds(i * block, block)
        copy = pltpu.make_async_copy(
            hidden_hbm.at[0, rows, :], hidden_ref.at[rows, :], hidden_sem.at[i]
        )
        copy.start()
        hidden_copies.append(copy)
    in_copies = []
    for i in range(units // in_chunk):
        columns = pl.ds(i * in_chunk, in_chunk)
        copy = pltpu.make_async_copy(
            in_weight_hbm.at[:, columns], in_weight_ref.at[:, columns], in_sem.at[i]
        )
        copy.start()
        in_copies.append(copy)
    out_copy = pltpu.make_async_copy(out_weight_hbm, out_weight_ref, out_sem)
    out_copy.start()

    def spaced_store(ref, first, values):
        for i in range(values.shape[0] // chips):
            ref[pl.ds(first + i, chips, stride=GROUP), :] = values[i * chips : (i + 1) * chips, :]

    used = half_rows // chips
    blank = jnp.zeros(((GROUP - used) * chips, LANES), f32)
    half = pl.ds(pl.multiple_of(side_ref[0] * half_rows, half_rows), half_rows)
    tall_ref[...] = jnp.zeros(tall_ref.shape, f32)
    tall_ref[:mel_bins, :] = noisy_ref[:, half]
    for i in range(half_rows // LANES):
        row = pl.ds(side_ref[0] * (half_rows // LANES) + i, 1)
        columns = slice(i * LANES, (i + 1) * LANES)
        tall_ref[mel_bins : mel_bins + 1, columns] = holder_ref[row, :].astype(f32)
        tall_ref[mel_bins + 1 : mel_bins + 2, columns] = jnp.where(
            position_ref[row, :] == 0, 1.0, 0.0
        )
    spaced_store(base_ref, 0, tall_ref[...].T)
    spaced_store(base_ref, used, blank)
    spaced_store(speed_ref.at[0], used, blank)
    spaced_store(speed_ref.at[1], used, blank)
    mel_pad_ref[...] = jnp.zeros(mel_pad_ref.shape, bf16)
    mel_pad_ref[:mel_bins, :] = mel_weight_ref[...]
    bias_pad_ref[...] = jnp.zeros(bias_pad_ref.shape, f32)
    bias_pad_ref[:, :mel_bins] = mel_bias_ref[...]

    scale = 1.0 + modulation_ref[1:2, :]
    for i in range(frames // block):
        hidden_copies[i].wait()
        for low in range(i * block, (i + 1) * block, 64):
            rows = slice(low, low + 64)
            normed = layer_norm(hidden_ref[rows, :].astype(f32)) * scale + modulation_ref[0:1, :]
            normed_ref[rows, :] = normed.astype(bf16)

    for j in range(units // in_chunk):
        columns = slice(j * in_chunk, (j + 1) * in_chunk)
        in_copies[j].wait()
        for i in range(frames // block):
            rows = slice(i * block, (i + 1) * block)
            inner = jnp.dot(
                normed_ref[rows, :], in_weight_ref[:, columns], preferred_element_type=f32
            )
            active_ref[rows, columns] = gelu_tanh(inner + in_bias_ref[:, columns]).astype(bf16)

    out_copy.wait()
    out_scale = 1.0 + modulation_ref[4:5, :]

    def finish(i):
        for low in range(i * tail, (i + 1) * tail, 64):
            rows = slice(low, low + 64)
            back = back_ref[i % 2, low - i * tail : low - i * tail + 64, :] + out_bias_ref[...]
            block_out = hidden_ref[rows, :].astype(f32) + modulation_ref[2:3, :] * back
            final = layer_norm(block_out) * out_scale + modulation_ref[3:4, :]
            normed_ref[rows, :] = final.astype(bf16)

    def emit(i):
        first = i * tail
        speed = nt_dot(normed_ref[first : first + tail, :], mel_pad_ref[...]) + bias_pad_ref[...]
        part = first // half_rows
        spaced_store(speed_ref.at[part], (first - part * half_rows) // chips, speed)

    count = frames // tail
    for i in range(count + 1):
        if i < count:
            back_ref[i % 2] = jnp.dot(
                active_ref[i * tail : (i + 1) * tail, :],
                out_weight_ref[...],
                preferred_element_type=f32,
            )
        if i > 0:
            finish(i - 1)
            emit(i - 1)

    @pl.when(side_ref[0] == 0)
    def _():
        own_ref[...] = speed_ref[0]
        sent_ref[...] = speed_ref[1]

    @pl.when(side_ref[0] != 0)
    def _():
        own_ref[...] = speed_ref[1]
        sent_ref[...] = speed_ref[0]


def velocity_halves(
    side,
    hidden,
    modulation,
    feedforward_in_weight,
    feedforward_in_bias,
    feedforward_out_weight,
    feedforward_out_bias,
    mel_velocity_weight,
    mel_velocity_bias,
    noisy_mel_state,
    frame_holder,
    frame_position,
    chips,
    block=384,
    tail=384,
    in_chunk=1024,
):
    frames, width = hidden.shape[1:]
    units = feedforward_in_weight.shape[1]
    f32, bf16 = jnp.float32, jnp.bfloat16
    spaced = jax.ShapeDtypeStruct((chips * GROUP, LANES), f32)
    vmem = pl.BlockSpec(memory_space=pltpu.VMEM)
    hbm = pl.BlockSpec(memory_space=pl.ANY)
    return pl.pallas_call(
        functools.partial(velocity_kernel, block=block, tail=tail, in_chunk=in_chunk),
        out_shape=(spaced,) * 3,
        in_specs=[pl.BlockSpec(memory_space=pltpu.SMEM), hbm, vmem, hbm, vmem, hbm] + [vmem] * 6,
        out_specs=(vmem,) * 3,
        scratch_shapes=[
            pltpu.VMEM((frames, width), bf16),
            pltpu.VMEM((width, units), bf16),
            pltpu.VMEM((units, width), bf16),
            pltpu.VMEM((LANES, width), bf16),
            pltpu.VMEM((1, LANES), f32),
            pltpu.VMEM((LANES, frames // 2), f32),
            pltpu.VMEM((frames, width), bf16),
            pltpu.VMEM((frames, units), bf16),
            pltpu.VMEM((2, chips * GROUP, LANES), f32),
            pltpu.VMEM((2, tail, width), f32),
            pltpu.SemaphoreType.DMA((frames // block,)),
            pltpu.SemaphoreType.DMA((units // in_chunk,)),
            pltpu.SemaphoreType.DMA(()),
        ],
        compiler_params=pltpu.CompilerParams(vmem_limit_bytes=60 * 1024 * 1024),
        name="velocity",
    )(
        side,
        hidden,
        modulation,
        feedforward_in_weight,
        feedforward_in_bias[None],
        feedforward_out_weight,
        feedforward_out_bias[None],
        mel_velocity_weight.T,
        mel_velocity_bias[None],
        noisy_mel_state,
        frame_holder.reshape(-1, LANES),
        frame_position.reshape(-1, LANES),
    )


SIN_TERMS = (
    3.141592579805583,
    -5.167706866168128,
    2.550031193522954,
    -0.5980441939334223,
    0.07721838619602994,
)


def snake_rows(signal, turns, inverse):
    half_turns = signal * turns
    part = half_turns - jnp.round(half_turns)
    square = part * part
    poly = SIN_TERMS[4] * square + SIN_TERMS[3]
    poly = poly * square + SIN_TERMS[2]
    poly = poly * square + SIN_TERMS[1]
    poly = poly * square + SIN_TERMS[0]
    sine = poly * part
    return signal + sine * sine * inverse


def vocoder_kernel(
    length_ref,
    arrived_ref,
    input_weight_ref,
    input_bias_ref,
    up_weight_hbm,
    up_bias_ref,
    freq_first_ref,
    dilated_weight_ref,
    dilated_bias_ref,
    freq_second_ref,
    second_weight_ref,
    second_bias_ref,
    wave_ref,
    mel_ref,
    taps_ref,
    shift_wide_ref,
    pre_ref,
    shift_ref,
    up_ref,
    first_ref,
    second_ref,
    out_ref,
    up_weight_ref,
    up_sem,
    even_ref,
    odd_ref,
    *,
    mel_bins,
    block,
):
    frames = up_ref.shape[1]
    piece_frames = out_ref.shape[1] // pl.num_programs(0)
    part_rows = arrived_ref.shape[0] // 2
    blocks = frames // block
    halo = 8
    f32, bf16 = jnp.float32, jnp.bfloat16
    step = pl.program_id(0)
    length = length_ref[0]

    def keep_rows(first, count):
        row = lax.broadcasted_iota(jnp.int32, (count, 1), 0) + first
        return row < length

    @pl.when(step == 0)
    def _():
        up_copy = pltpu.make_async_copy(up_weight_hbm, up_weight_ref, up_sem)
        up_copy.start()
        arrived = arrived_ref[...]

        def shard_row(shape, axis):
            i = lax.broadcasted_iota(jnp.int32, shape, axis)
            side = (i >= part_rows).astype(jnp.int32)
            inner = i - side * part_rows
            turn = lax.rem(inner, GROUP)
            row = side * (frames // 2) + turn * (part_rows // GROUP) + inner // GROUP
            return jnp.where(turn < frames * GROUP // (2 * part_rows), row, -4 * frames)

        lane = lax.broadcasted_iota(jnp.int32, arrived.shape, 1)
        flagged = jnp.where(lane == mel_bins + 1, arrived.astype(f32), 0.0)
        start = jnp.sum(
            jnp.where(flagged > 0.5, shard_row(arrived.shape, 0).astype(f32), 0.0), keepdims=True
        ).astype(jnp.int32)
        mel_ref[...] = jnp.zeros(mel_ref.shape, f32)
        turned = shard_row((1, arrived.shape[0]), 1) - start
        for i in range(frames // 128):
            ahead = turned - i * 128 - lax.broadcasted_iota(jnp.int32, (128, 1), 0)
            pick = ((ahead == 0) | (ahead == -frames)).astype(bf16)
            mel_ref[halo + i * 128 : halo + (i + 1) * 128, :] = jnp.dot(
                pick, arrived, preferred_element_type=f32
            )
        for k in range(KPRE):
            low = halo + k - KPRE // 2
            taps_ref[:, k * LANES : (k + 1) * LANES] = mel_ref[low : low + frames, :].astype(bf16)
        shift_wide_ref[...] = jnp.zeros(shift_wide_ref.shape, f32)
        for i in range(blocks):
            rows = slice(i * block, (i + 1) * block)
            pre = jnp.dot(taps_ref[rows, :], input_weight_ref[...], preferred_element_type=f32)
            pre = jnp.where(keep_rows(i * block, block), pre + input_bias_ref[...], 0.0)
            shift_wide_ref[halo + i * block : halo + (i + 1) * block, :] = pre
        for k in range(3):
            low = halo + k - 1
            pre_ref[k] = shift_wide_ref[low : low + frames, :].astype(bf16)
        shift_ref[...] = jnp.zeros(shift_ref.shape, f32)

        turns_first = freq_first_ref[...] * (1.0 / math.pi)
        inverse_first = 1.0 / freq_first_ref[...]
        turns_second = freq_second_ref[...] * (1.0 / math.pi)
        inverse_second = 1.0 / freq_second_ref[...]

        def neighbour_rows(offset):
            low = halo + offset
            return shift_ref[low : low + frames, :].astype(bf16)

        up_copy.wait()

        def pipeline(product, finish):
            for i in range(blocks):
                rows = slice(i * block, (i + 1) * block)
                even_ref[rows, :] = product(0, rows)

            @pl.loop(0, UP // 2)
            def _(pair):
                for r, ready_ref, r_next, next_ref in (
                    (2 * pair, even_ref, 2 * pair + 1, odd_ref),
                    (2 * pair + 1, odd_ref, jnp.minimum(2 * pair + 2, UP - 1), even_ref),
                ):
                    for i in range(blocks):
                        rows = slice(i * block, (i + 1) * block)
                        next_ref[rows, :] = product(r_next, rows)
                        for low in range(i * block, (i + 1) * block, 64):
                            finish(r, low, ready_ref[low : low + 64, :])

        def up_product(r, rows):
            side = jnp.where(r < UP // 2, 0, 2)
            return nt_dot(
                jnp.concatenate([pre_ref[1, rows, :], pre_ref[side, rows, :]], axis=1),
                jnp.concatenate(
                    [up_weight_ref[r + UP // 2], up_weight_ref[lax.rem(r + UP // 2 + UP, KT)]],
                    axis=1,
                ),
            )

        def up_finish(r, low, up):
            rows = slice(low, low + 64)
            up = jnp.where(keep_rows(low, 64), up + up_bias_ref[...], 0.0)
            up = up.astype(bf16)
            up_ref[r, rows, :] = up
            first = snake_rows(up.astype(f32), turns_first, inverse_first)
            first_ref[r + 3, rows, :] = first.astype(bf16)

        pipeline(up_product, up_finish)

        for r in range(DILATION_RATE):
            shift_ref[halo : halo + frames, :] = first_ref[r + 3].astype(f32)
            first_ref[r + 3 + UP] = neighbour_rows(1)
        for r in range(UP - DILATION_RATE, UP):
            shift_ref[halo : halo + frames, :] = first_ref[r + 3].astype(f32)
            first_ref[r + 3 - UP] = neighbour_rows(-1)

        def inner_product(r, rows):
            around = [first_ref[r + DILATION_RATE * k, rows, :] for k in range(3)]
            return jnp.dot(
                jnp.concatenate(around, axis=1),
                dilated_weight_ref[...],
                preferred_element_type=f32,
            )

        def inner_finish(r, low, inner):
            inner = jnp.where(keep_rows(low, 64), inner + dilated_bias_ref[...], 0.0)
            second = snake_rows(inner, turns_second, inverse_second)
            second_ref[r + 1, low : low + 64, :] = second.astype(bf16)

        pipeline(inner_product, inner_finish)

        shift_ref[halo : halo + frames, :] = second_ref[1].astype(f32)
        second_ref[UP + 1] = neighbour_rows(1)
        shift_ref[halo : halo + frames, :] = second_ref[UP].astype(f32)
        second_ref[0] = neighbour_rows(-1)

        def outer_product(r, rows):
            around = [second_ref[r + k, rows, :] for k in range(3)]
            return jnp.dot(
                jnp.concatenate(around, axis=1),
                second_weight_ref[...],
                preferred_element_type=f32,
            )

        def outer_finish(r, low, outer):
            rows = slice(low, low + 64)
            outer = jnp.where(keep_rows(low, 64), outer + second_bias_ref[...], 0.0)
            out_ref[r, rows, :] = (up_ref[r, rows, :].astype(f32) + outer).astype(bf16)

        pipeline(outer_product, outer_finish)

    base = pl.multiple_of(step * piece_frames, piece_frames)
    narrow = 256 // UP
    row = lax.broadcasted_iota(jnp.int32, (256, 256), 0)
    col = lax.broadcasted_iota(jnp.int32, (256, 256), 1)
    weave = (col == lax.rem(row, narrow) * UP + row // narrow).astype(bf16)
    for piece in range(piece_frames // narrow):
        rows = pl.ds(base + piece * narrow, narrow)
        phases = jnp.concatenate([out_ref[r, rows, :] for r in range(UP)], axis=0)
        woven = lax.dot_general(
            phases, weave, (((0,), (0,)), ((), ())), preferred_element_type=f32
        )
        wave_ref[0, :, piece * 256 : (piece + 1) * 256] = woven.astype(bf16)


def vocoder(
    arrived,
    length,
    mel_bins,
    input_conv_weight,
    input_conv_bias,
    transposed_conv_weight,
    transposed_conv_bias,
    snake_freq_first,
    dilated_conv_weight,
    dilated_conv_bias,
    snake_freq_second,
    second_conv_weight,
    second_conv_bias,
    frames,
    block=256,
    piece=256,
):
    wide = input_conv_bias.shape[0]
    channels = transposed_conv_bias.shape[0]
    f32, bf16 = jnp.float32, jnp.bfloat16
    taps_weight = jnp.pad(
        input_conv_weight.reshape(KPRE, mel_bins, wide), ((0, 0), (0, LANES - mel_bins), (0, 0))
    ).reshape(KPRE * LANES, wide)
    operands = [
        arrived,
        taps_weight,
        input_conv_bias[None],
        transposed_conv_weight.reshape(KT, channels, wide),
        transposed_conv_bias[None],
        snake_freq_first[None],
        dilated_conv_weight,
        dilated_conv_bias[None],
        snake_freq_second[None],
        second_conv_weight,
        second_conv_bias[None],
    ]
    return pl.pallas_call(
        functools.partial(vocoder_kernel, mel_bins=mel_bins, block=block),
        out_shape=jax.ShapeDtypeStruct((1, channels, frames * UP), bf16),
        grid=(frames // piece,),
        in_specs=[pl.BlockSpec(memory_space=pltpu.SMEM)]
        + [
            pl.BlockSpec(memory_space=pl.ANY)
            if x.ndim == 3 and x.shape[0] == KT
            else pl.BlockSpec(x.shape, lambda i, n=x.ndim: (0,) * n, pipeline_mode=pl.Buffered(1))
            for x in operands
        ],
        out_specs=pl.BlockSpec((1, channels, piece * UP), lambda i: (0, 0, i)),
        scratch_shapes=[
            pltpu.VMEM((frames + 16, LANES), f32),
            pltpu.VMEM((frames, KPRE * LANES), bf16),
            pltpu.VMEM((frames + 16, wide), f32),
            pltpu.VMEM((3, frames, wide), bf16),
            pltpu.VMEM((frames + 16, channels), f32),
            pltpu.VMEM((UP, frames, channels), bf16),
            pltpu.VMEM((UP + 6, frames, channels), bf16),
            pltpu.VMEM((UP + 2, frames, channels), bf16),
            pltpu.VMEM((UP, frames, channels), bf16),
            pltpu.VMEM((KT, channels, wide), bf16),
            pltpu.SemaphoreType.DMA(()),
            pltpu.VMEM((frames, channels), f32),
            pltpu.VMEM((frames, channels), f32),
        ],
        compiler_params=pltpu.CompilerParams(vmem_limit_bytes=60 * 1024 * 1024),
        name="vocoder",
    )(length, *operands)


def local(
    hidden,
    noisy_mel_state,
    modulation,
    feedforward_in_weight,
    feedforward_in_bias,
    feedforward_out_weight,
    feedforward_out_bias,
    mel_velocity_weight,
    mel_velocity_bias,
    input_conv_weight,
    input_conv_bias,
    transposed_conv_weight,
    transposed_conv_bias,
    snake_freq_first,
    dilated_conv_weight,
    dilated_conv_bias,
    snake_freq_second,
    second_conv_weight,
    second_conv_bias,
    frame_holder,
    frame_position,
    holder_utterance_length,
):
    step_size = math.cos(0.5 * math.pi * (NFE - 1) / NFE)
    chips = lax.axis_size("seq")
    owners = lax.axis_size("branch") * chips
    mel_bins, frames = noisy_mel_state.shape
    branch_side = lax.axis_index("branch").astype(jnp.int32)
    own_half, sent_half, base = velocity_halves(
        branch_side[None],
        hidden,
        modulation,
        feedforward_in_weight,
        feedforward_in_bias,
        feedforward_out_weight,
        feedforward_out_bias,
        mel_velocity_weight,
        mel_velocity_bias,
        noisy_mel_state,
        frame_holder,
        frame_position,
        chips,
    )
    peer_half = lax.ppermute(sent_half, "branch", [(0, 1), (1, 0)])
    conditional = jnp.where(branch_side == 0, own_half, peer_half)
    unconditional = jnp.where(branch_side == 0, peer_half, own_half)
    guided = (1.0 + GUIDE) * conditional - GUIDE * unconditional
    packed = (base + step_size * guided).astype(jnp.bfloat16)
    spread = lax.all_to_all(packed.reshape(chips, GROUP, LANES), "seq", 0, 0, tiled=True)
    rows = spread.reshape(chips * GROUP, LANES)
    owner_of = rows[:, mel_bins].astype(jnp.int32)
    slot_of = owner_of * GROUP + jnp.arange(chips * GROUP, dtype=jnp.int32) % GROUP
    onehot = (slot_of[:, None] == jnp.arange(owners * GROUP, dtype=jnp.int32)[None, :]).astype(
        jnp.bfloat16
    )
    slots = lax.dot_general(
        onehot, rows, (((0,), (0,)), ((), ())), preferred_element_type=jnp.float32
    ).astype(jnp.bfloat16)
    arrived = lax.all_to_all(
        slots.reshape(owners, GROUP, LANES), ("branch", "seq"), 0, 0, tiled=True
    ).reshape(owners * GROUP, LANES)
    self_owner = lax.axis_index(("branch", "seq"))
    length = lax.dynamic_slice_in_dim(holder_utterance_length, self_owner, 1, 0)
    return vocoder(
        arrived,
        length,
        mel_bins,
        input_conv_weight,
        input_conv_bias,
        transposed_conv_weight,
        transposed_conv_bias,
        snake_freq_first,
        dilated_conv_weight,
        dilated_conv_bias,
        snake_freq_second,
        second_conv_weight,
        second_conv_bias,
        frames,
    )


def solution(mesh):
    return jax.shard_map(
        local,
        mesh=mesh,
        in_specs=(
            P("branch", "seq", None),
            P(None, "seq"),
            P(),
            P(),
            P(),
            P(),
            P(),
            P(),
            P(),
            P(),
            P(),
            P(),
            P(),
            P(),
            P(),
            P(),
            P(),
            P(),
            P(),
            P("seq"),
            P("seq"),
            P(),
        ),
        out_specs=P(("branch", "seq"), None, None),
        check_vma=False,
    )
```

```python
import functools
import math

import jax
import jax.numpy as jnp
from jax import lax
from jax.experimental import pallas as pl
from jax.experimental.pallas import tpu as pltpu
from jax.sharding import PartitionSpec as P

UP = 8
KT = 16
KPRE = 7
DILATION_RATE = 3
NFE = 16


GUIDE = 2.0
LANES = 128
GROUP = 8
GELU_SCALE = math.sqrt(2.0 / math.pi)


def layer_norm(row_block):
    row_mean = jnp.mean(row_block, axis=-1, keepdims=True)
    centred = row_block - row_mean
    row_var = jnp.mean(centred * centred, axis=-1, keepdims=True)
    return centred * lax.rsqrt(row_var + 1e-06)


def gelu_tanh(inner):
    slope = inner * (GELU_SCALE + (GELU_SCALE * 0.044715) * (inner * inner))
    half = 0.5 * inner
    return half + half * jnp.tanh(slope)


def nt_dot(left, right):
    return lax.dot_general(
        left, right, (((1,), (1,)), ((), ())), preferred_element_type=jnp.float32
    )


def velocity_kernel(
    side_ref,
    hidden_hbm,
    modulation_ref,
    in_weight_hbm,
    in_bias_ref,
    out_weight_hbm,
    out_bias_ref,
    mel_weight_ref,
    mel_bias_ref,
    noisy_ref,
    holder_ref,
    position_ref,
    own_ref,
    sent_ref,
    base_ref,
    hidden_ref,
    in_weight_ref,
    out_weight_ref,
    mel_pad_ref,
    bias_pad_ref,
    tall_ref,
    normed_ref,
    active_ref,
    speed_ref,
    back_ref,
    hidden_sem,
    in_sem,
    out_sem,
    *,
    block,
    tail,
    in_chunk,
):
    frames, width = hidden_ref.shape
    units = in_weight_ref.shape[1]
    half_rows = frames // 2
    mel_bins = noisy_ref.shape[0]
    chips = own_ref.shape[0] // GROUP
    f32, bf16 = jnp.float32, jnp.bfloat16
    hidden_copies = []
    for i in range(frames // block):
        rows = pl.ds(i * block, block)
        copy = pltpu.make_async_copy(
            hidden_hbm.at[0, rows, :], hidden_ref.at[rows, :], hidden_sem.at[i]
        )
        copy.start()
        hidden_copies.append(copy)
    in_copies = []
    for i in range(units // in_chunk):
        columns = pl.ds(i * in_chunk, in_chunk)
        copy = pltpu.make_async_copy(
            in_weight_hbm.at[:, columns], in_weight_ref.at[:, columns], in_sem.at[i]
        )
        copy.start()
        in_copies.append(copy)
    out_copy = pltpu.make_async_copy(out_weight_hbm, out_weight_ref, out_sem)
    out_copy.start()

    def spaced_store(ref, first, values):
        for i in range(values.shape[0] // chips):
            ref[pl.ds(first + i, chips, stride=GROUP), :] = values[i * chips : (i + 1) * chips, :]

    used = half_rows // chips
    blank = jnp.zeros(((GROUP - used) * chips, LANES), f32)
    half = pl.ds(pl.multiple_of(side_ref[0] * half_rows, half_rows), half_rows)
    tall_ref[...] = jnp.zeros(tall_ref.shape, f32)
    tall_ref[:mel_bins, :] = noisy_ref[:, half]
    for i in range(half_rows // LANES):
        row = pl.ds(side_ref[0] * (half_rows // LANES) + i, 1)
        columns = slice(i * LANES, (i + 1) * LANES)
        tall_ref[mel_bins : mel_bins + 1, columns] = holder_ref[row, :].astype(f32)
        tall_ref[mel_bins + 1 : mel_bins + 2, columns] = jnp.where(
            position_ref[row, :] == 0, 1.0, 0.0
        )
    spaced_store(base_ref, 0, tall_ref[...].T)
    spaced_store(base_ref, used, blank)
    spaced_store(speed_ref.at[0], used, blank)
    spaced_store(speed_ref.at[1], used, blank)
    mel_pad_ref[...] = jnp.zeros(mel_pad_ref.shape, bf16)
    mel_pad_ref[:mel_bins, :] = mel_weight_ref[...]
    bias_pad_ref[...] = jnp.zeros(bias_pad_ref.shape, f32)
    bias_pad_ref[:, :mel_bins] = mel_bias_ref[...]

    scale = 1.0 + modulation_ref[1:2, :]
    for i in range(frames // block):
        hidden_copies[i].wait()
        for low in range(i * block, (i + 1) * block, 64):
            rows = slice(low, low + 64)
            normed = layer_norm(hidden_ref[rows, :].astype(f32)) * scale + modulation_ref[0:1, :]
            normed_ref[rows, :] = normed.astype(bf16)

    for j in range(units // in_chunk):
        columns = slice(j * in_chunk, (j + 1) * in_chunk)
        in_copies[j].wait()
        for i in range(frames // block):
            rows = slice(i * block, (i + 1) * block)
            inner = jnp.dot(
                normed_ref[rows, :], in_weight_ref[:, columns], preferred_element_type=f32
            )
            active_ref[rows, columns] = gelu_tanh(inner + in_bias_ref[:, columns]).astype(bf16)

    out_copy.wait()
    out_scale = 1.0 + modulation_ref[4:5, :]

    def finish(i):
        for low in range(i * tail, (i + 1) * tail, 64):
            rows = slice(low, low + 64)
            back = back_ref[i % 2, low - i * tail : low - i * tail + 64, :] + out_bias_ref[...]
            block_out = hidden_ref[rows, :].astype(f32) + modulation_ref[2:3, :] * back
            final = layer_norm(block_out) * out_scale + modulation_ref[3:4, :]
            normed_ref[rows, :] = final.astype(bf16)

    def emit(i):
        first = i * tail
        speed = nt_dot(normed_ref[first : first + tail, :], mel_pad_ref[...]) + bias_pad_ref[...]
        part = first // half_rows
        spaced_store(speed_ref.at[part], (first - part * half_rows) // chips, speed)

    count = frames // tail
    for i in range(count + 1):
        if i < count:
            back_ref[i % 2] = jnp.dot(
                active_ref[i * tail : (i + 1) * tail, :],
                out_weight_ref[...],
                preferred_element_type=f32,
            )
        if i > 0:
            finish(i - 1)
            emit(i - 1)

    @pl.when(side_ref[0] == 0)
    def _():
        own_ref[...] = speed_ref[0]
        sent_ref[...] = speed_ref[1]

    @pl.when(side_ref[0] != 0)
    def _():
        own_ref[...] = speed_ref[1]
        sent_ref[...] = speed_ref[0]


def velocity_halves(
    side,
    hidden,
    modulation,
    feedforward_in_weight,
    feedforward_in_bias,
    feedforward_out_weight,
    feedforward_out_bias,
    mel_velocity_weight,
    mel_velocity_bias,
    noisy_mel_state,
    frame_holder,
    frame_position,
    chips,
    block=384,
    tail=384,
    in_chunk=1024,
):
    frames, width = hidden.shape[1:]
    units = feedforward_in_weight.shape[1]
    f32, bf16 = jnp.float32, jnp.bfloat16
    spaced = jax.ShapeDtypeStruct((chips * GROUP, LANES), f32)
    vmem = pl.BlockSpec(memory_space=pltpu.VMEM)
    hbm = pl.BlockSpec(memory_space=pl.ANY)
    return pl.pallas_call(
        functools.partial(velocity_kernel, block=block, tail=tail, in_chunk=in_chunk),
        out_shape=(spaced,) * 3,
        in_specs=[pl.BlockSpec(memory_space=pltpu.SMEM), hbm, vmem, hbm, vmem, hbm] + [vmem] * 6,
        out_specs=(vmem,) * 3,
        scratch_shapes=[
            pltpu.VMEM((frames, width), bf16),
            pltpu.VMEM((width, units), bf16),
            pltpu.VMEM((units, width), bf16),
            pltpu.VMEM((LANES, width), bf16),
            pltpu.VMEM((1, LANES), f32),
            pltpu.VMEM((LANES, frames // 2), f32),
            pltpu.VMEM((frames, width), bf16),
            pltpu.VMEM((frames, units), bf16),
            pltpu.VMEM((2, chips * GROUP, LANES), f32),
            pltpu.VMEM((2, tail, width), f32),
            pltpu.SemaphoreType.DMA((frames // block,)),
            pltpu.SemaphoreType.DMA((units // in_chunk,)),
            pltpu.SemaphoreType.DMA(()),
        ],
        compiler_params=pltpu.CompilerParams(vmem_limit_bytes=60 * 1024 * 1024),
        name="velocity",
    )(
        side,
        hidden,
        modulation,
        feedforward_in_weight,
        feedforward_in_bias[None],
        feedforward_out_weight,
        feedforward_out_bias[None],
        mel_velocity_weight.T,
        mel_velocity_bias[None],
        noisy_mel_state,
        frame_holder.reshape(-1, LANES),
        frame_position.reshape(-1, LANES),
    )


SIN_TERMS = (
    3.141592579805583,
    -5.167706866168128,
    2.550031193522954,
    -0.5980441939334223,
    0.07721838619602994,
)


def snake_rows(signal, turns, inverse):
    half_turns = signal * turns
    part = half_turns - jnp.round(half_turns)
    square = part * part
    poly = SIN_TERMS[4] * square + SIN_TERMS[3]
    poly = poly * square + SIN_TERMS[2]
    poly = poly * square + SIN_TERMS[1]
    poly = poly * square + SIN_TERMS[0]
    sine = poly * part
    return signal + sine * sine * inverse


def vocoder_kernel(
    length_ref,
    arrived_ref,
    input_weight_ref,
    input_bias_ref,
    up_weight_hbm,
    up_bias_ref,
    freq_first_ref,
    dilated_weight_ref,
    dilated_bias_ref,
    freq_second_ref,
    second_weight_ref,
    second_bias_ref,
    wave_hbm,
    mel_ref,
    taps_ref,
    shift_wide_ref,
    pre_ref,
    shift_ref,
    up_ref,
    first_ref,
    second_ref,
    out_ref,
    up_weight_ref,
    up_sem,
    even_ref,
    odd_ref,
    wave_ref,
    wave_sem,
    *,
    mel_bins,
    block,
):
    frames = up_ref.shape[1]
    part_rows = arrived_ref.shape[0] // 2
    blocks = frames // block
    halo = 8
    f32, bf16 = jnp.float32, jnp.bfloat16
    length = length_ref[0]

    def keep_rows(first, count):
        row = lax.broadcasted_iota(jnp.int32, (count, 1), 0) + first
        return row < length

    up_copy = pltpu.make_async_copy(up_weight_hbm, up_weight_ref, up_sem)
    up_copy.start()
    arrived = arrived_ref[...]

    def shard_row(shape, axis):
        i = lax.broadcasted_iota(jnp.int32, shape, axis)
        side = (i >= part_rows).astype(jnp.int32)
        inner = i - side * part_rows
        turn = lax.rem(inner, GROUP)
        row = side * (frames // 2) + turn * (part_rows // GROUP) + inner // GROUP
        return jnp.where(turn < frames * GROUP // (2 * part_rows), row, -4 * frames)

    lane = lax.broadcasted_iota(jnp.int32, arrived.shape, 1)
    flagged = jnp.where(lane == mel_bins + 1, arrived.astype(f32), 0.0)
    start = jnp.sum(
        jnp.where(flagged > 0.5, shard_row(arrived.shape, 0).astype(f32), 0.0), keepdims=True
    ).astype(jnp.int32)
    mel_ref[...] = jnp.zeros(mel_ref.shape, f32)
    turned = shard_row((1, arrived.shape[0]), 1) - start
    for i in range(frames // 128):
        ahead = turned - i * 128 - lax.broadcasted_iota(jnp.int32, (128, 1), 0)
        pick = ((ahead == 0) | (ahead == -frames)).astype(bf16)
        mel_ref[halo + i * 128 : halo + (i + 1) * 128, :] = jnp.dot(
            pick, arrived, preferred_element_type=f32
        )
    for k in range(KPRE):
        low = halo + k - KPRE // 2
        taps_ref[:, k * LANES : (k + 1) * LANES] = mel_ref[low : low + frames, :].astype(bf16)
    shift_wide_ref[...] = jnp.zeros(shift_wide_ref.shape, f32)
    for i in range(blocks):
        rows = slice(i * block, (i + 1) * block)
        pre = jnp.dot(taps_ref[rows, :], input_weight_ref[...], preferred_element_type=f32)
        pre = jnp.where(keep_rows(i * block, block), pre + input_bias_ref[...], 0.0)
        shift_wide_ref[halo + i * block : halo + (i + 1) * block, :] = pre
    for k in range(3):
        low = halo + k - 1
        pre_ref[k] = shift_wide_ref[low : low + frames, :].astype(bf16)
    shift_ref[...] = jnp.zeros(shift_ref.shape, f32)

    turns_first = freq_first_ref[...] * (1.0 / math.pi)
    inverse_first = 1.0 / freq_first_ref[...]
    turns_second = freq_second_ref[...] * (1.0 / math.pi)
    inverse_second = 1.0 / freq_second_ref[...]

    def neighbour_rows(offset):
        low = halo + offset
        return shift_ref[low : low + frames, :].astype(bf16)

    up_copy.wait()

    def pipeline(product, finish):
        for i in range(blocks):
            rows = slice(i * block, (i + 1) * block)
            even_ref[rows, :] = product(0, rows)

        for r in range(UP):
            ready_ref, next_ref = (even_ref, odd_ref) if r % 2 == 0 else (odd_ref, even_ref)
            for i in range(blocks):
                rows = slice(i * block, (i + 1) * block)
                if r + 1 < UP:
                    next_ref[rows, :] = product(r + 1, rows)
                for low in range(i * block, (i + 1) * block, 64):
                    finish(r, low, ready_ref[low : low + 64, :])

    def up_product(r, rows):
        side = 0 if r < UP // 2 else 2
        return jnp.dot(
            jnp.concatenate([pre_ref[1, rows, :], pre_ref[side, rows, :]], axis=1),
            jnp.concatenate(
                [up_weight_ref[r + UP // 2], up_weight_ref[(r + UP // 2 + UP) % KT]],
                axis=0,
            ),
            preferred_element_type=f32,
        )

    def up_finish(r, low, up):
        rows = slice(low, low + 64)
        up = jnp.where(keep_rows(low, 64), up + up_bias_ref[...], 0.0)
        up = up.astype(bf16)
        up_ref[r, rows, :] = up
        first = snake_rows(up.astype(f32), turns_first, inverse_first)
        first_ref[r + 3, rows, :] = first.astype(bf16)

    pipeline(up_product, up_finish)

    for r in range(DILATION_RATE):
        shift_ref[halo : halo + frames, :] = first_ref[r + 3].astype(f32)
        first_ref[r + 3 + UP] = neighbour_rows(1)
    for r in range(UP - DILATION_RATE, UP):
        shift_ref[halo : halo + frames, :] = first_ref[r + 3].astype(f32)
        first_ref[r + 3 - UP] = neighbour_rows(-1)

    def inner_product(r, rows):
        around = [first_ref[r + DILATION_RATE * k, rows, :] for k in range(3)]
        return jnp.dot(
            jnp.concatenate(around, axis=1),
            dilated_weight_ref[...],
            preferred_element_type=f32,
        )

    def inner_finish(r, low, inner):
        inner = jnp.where(keep_rows(low, 64), inner + dilated_bias_ref[...], 0.0)
        second = snake_rows(inner, turns_second, inverse_second)
        second_ref[r + 1, low : low + 64, :] = second.astype(bf16)

    pipeline(inner_product, inner_finish)

    shift_ref[halo : halo + frames, :] = second_ref[1].astype(f32)
    second_ref[UP + 1] = neighbour_rows(1)
    shift_ref[halo : halo + frames, :] = second_ref[UP].astype(f32)
    second_ref[0] = neighbour_rows(-1)

    narrow = 256 // UP
    row = lax.broadcasted_iota(jnp.int32, (256, 256), 0)
    col = lax.broadcasted_iota(jnp.int32, (256, 256), 1)
    weave = (col == lax.rem(row, narrow) * UP + row // narrow).astype(bf16)

    def outer_product(low):
        for r in range(UP):
            around = [second_ref[r + k, low : low + 128, :] for k in range(3)]
            outer = jnp.dot(
                jnp.concatenate(around, axis=1),
                second_weight_ref[...],
                preferred_element_type=f32,
            )
            outer = jnp.where(keep_rows(low, 128), outer + second_bias_ref[...], 0.0)
            up = up_ref[r, low : low + 128, :].astype(f32)
            out_ref[r, low : low + 128, :] = (up + outer).astype(bf16)

    copies = []

    def woven(low):
        for first in range(low, low + 128, narrow):
            phases = jnp.concatenate(
                [out_ref[r, first : first + narrow, :] for r in range(UP)], axis=0
            )
            samples = lax.dot_general(
                phases, weave, (((0,), (0,)), ((), ())), preferred_element_type=f32
            )
            wave_ref[:, first * UP : (first + narrow) * UP] = samples.astype(bf16)
        columns = pl.ds(low * UP, 128 * UP)
        copy = pltpu.make_async_copy(
            wave_ref.at[:, columns], wave_hbm.at[0, :, columns], wave_sem.at[low // 128]
        )
        copy.start()
        copies.append(copy)

    for low in range(0, frames + 128, 128):
        if low < frames:
            outer_product(low)
        if low > 0:
            woven(low - 128)
    for copy in copies:
        copy.wait()


def vocoder(
    arrived,
    length,
    mel_bins,
    input_conv_weight,
    input_conv_bias,
    transposed_conv_weight,
    transposed_conv_bias,
    snake_freq_first,
    dilated_conv_weight,
    dilated_conv_bias,
    snake_freq_second,
    second_conv_weight,
    second_conv_bias,
    frames,
    block=128,
):
    wide = input_conv_bias.shape[0]
    channels = transposed_conv_bias.shape[0]
    f32, bf16 = jnp.float32, jnp.bfloat16
    taps_weight = jnp.pad(
        input_conv_weight.reshape(KPRE, mel_bins, wide), ((0, 0), (0, LANES - mel_bins), (0, 0))
    ).reshape(KPRE * LANES, wide)
    operands = [
        arrived,
        taps_weight,
        input_conv_bias[None],
        transposed_conv_weight.reshape(KT, channels, wide).transpose(0, 2, 1),
        transposed_conv_bias[None],
        snake_freq_first[None],
        dilated_conv_weight,
        dilated_conv_bias[None],
        snake_freq_second[None],
        second_conv_weight,
        second_conv_bias[None],
    ]
    return pl.pallas_call(
        functools.partial(vocoder_kernel, mel_bins=mel_bins, block=block),
        out_shape=jax.ShapeDtypeStruct((1, channels, frames * UP), bf16),
        in_specs=[pl.BlockSpec(memory_space=pltpu.SMEM)]
        + [
            pl.BlockSpec(memory_space=pl.ANY)
            if x.ndim == 3 and x.shape[0] == KT
            else pl.BlockSpec(memory_space=pltpu.VMEM)
            for x in operands
        ],
        out_specs=pl.BlockSpec(memory_space=pl.ANY),
        scratch_shapes=[
            pltpu.VMEM((frames + 16, LANES), f32),
            pltpu.VMEM((frames, KPRE * LANES), bf16),
            pltpu.VMEM((frames + 16, wide), f32),
            pltpu.VMEM((3, frames, wide), bf16),
            pltpu.VMEM((frames + 16, channels), f32),
            pltpu.VMEM((UP, frames, channels), bf16),
            pltpu.VMEM((UP + 6, frames, channels), bf16),
            pltpu.VMEM((UP + 2, frames, channels), bf16),
            pltpu.VMEM((UP, frames, channels), bf16),
            pltpu.VMEM((KT, wide, channels), bf16),
            pltpu.SemaphoreType.DMA(()),
            pltpu.VMEM((frames, channels), f32),
            pltpu.VMEM((frames, channels), f32),
            pltpu.VMEM((channels, frames * UP), bf16),
            pltpu.SemaphoreType.DMA((frames // 128,)),
        ],
        compiler_params=pltpu.CompilerParams(vmem_limit_bytes=60 * 1024 * 1024),
        name="vocoder",
    )(length, *operands)


def local(
    hidden,
    noisy_mel_state,
    modulation,
    feedforward_in_weight,
    feedforward_in_bias,
    feedforward_out_weight,
    feedforward_out_bias,
    mel_velocity_weight,
    mel_velocity_bias,
    input_conv_weight,
    input_conv_bias,
    transposed_conv_weight,
    transposed_conv_bias,
    snake_freq_first,
    dilated_conv_weight,
    dilated_conv_bias,
    snake_freq_second,
    second_conv_weight,
    second_conv_bias,
    frame_holder,
    frame_position,
    holder_utterance_length,
):
    step_size = math.cos(0.5 * math.pi * (NFE - 1) / NFE)
    chips = lax.axis_size("seq")
    owners = lax.axis_size("branch") * chips
    mel_bins, frames = noisy_mel_state.shape
    branch_side = lax.axis_index("branch").astype(jnp.int32)
    own_half, sent_half, base = velocity_halves(
        branch_side[None],
        hidden,
        modulation,
        feedforward_in_weight,
        feedforward_in_bias,
        feedforward_out_weight,
        feedforward_out_bias,
        mel_velocity_weight,
        mel_velocity_bias,
        noisy_mel_state,
        frame_holder,
        frame_position,
        chips,
    )
    peer_half = lax.ppermute(sent_half, "branch", [(0, 1), (1, 0)])
    conditional = jnp.where(branch_side == 0, own_half, peer_half)
    unconditional = jnp.where(branch_side == 0, peer_half, own_half)
    guided = (1.0 + GUIDE) * conditional - GUIDE * unconditional
    packed = (base + step_size * guided).astype(jnp.bfloat16)
    spread = lax.all_to_all(packed.reshape(chips, GROUP, LANES), "seq", 0, 0, tiled=True)
    rows = spread.reshape(chips * GROUP, LANES)
    owner_of = rows[:, mel_bins].astype(jnp.int32)
    slot_of = owner_of * GROUP + jnp.arange(chips * GROUP, dtype=jnp.int32) % GROUP
    onehot = (slot_of[:, None] == jnp.arange(owners * GROUP, dtype=jnp.int32)[None, :]).astype(
        jnp.bfloat16
    )
    slots = lax.dot_general(
        onehot, rows, (((0,), (0,)), ((), ())), preferred_element_type=jnp.float32
    ).astype(jnp.bfloat16)
    arrived = lax.all_to_all(
        slots.reshape(owners, GROUP, LANES), ("branch", "seq"), 0, 0, tiled=True
    ).reshape(owners * GROUP, LANES)
    self_owner = lax.axis_index(("branch", "seq"))
    length = lax.dynamic_slice_in_dim(holder_utterance_length, self_owner, 1, 0)
    return vocoder(
        arrived,
        length,
        mel_bins,
        input_conv_weight,
        input_conv_bias,
        transposed_conv_weight,
        transposed_conv_bias,
        snake_freq_first,
        dilated_conv_weight,
        dilated_conv_bias,
        snake_freq_second,
        second_conv_weight,
        second_conv_bias,
        frames,
    )


def solution(mesh):
    return jax.shard_map(
        local,
        mesh=mesh,
        in_specs=(
            P("branch", "seq", None),
            P(None, "seq"),
            P(),
            P(),
            P(),
            P(),
            P(),
            P(),
            P(),
            P(),
            P(),
            P(),
            P(),
            P(),
            P(),
            P(),
            P(),
            P(),
            P(),
            P("seq"),
            P("seq"),
            P(),
        ),
        out_specs=P(("branch", "seq"), None, None),
        check_vma=False,
    )
```

```python
import functools
import math

import jax
import jax.numpy as jnp
from jax import lax
from jax.experimental import pallas as pl
from jax.experimental.pallas import tpu as pltpu
from jax.sharding import PartitionSpec as P

UP = 8
KT = 16
KPRE = 7
DILATION_RATE = 3
NFE = 16


GUIDE = 2.0
LANES = 128
GROUP = 8
GELU_SCALE = math.sqrt(2.0 / math.pi)


def layer_norm(row_block):
    row_mean = jnp.mean(row_block, axis=-1, keepdims=True)
    centred = row_block - row_mean
    row_var = jnp.mean(centred * centred, axis=-1, keepdims=True)
    return centred * lax.rsqrt(row_var + 1e-06)


def gelu_tanh(inner):
    slope = inner * (GELU_SCALE + (GELU_SCALE * 0.044715) * (inner * inner))
    half = 0.5 * inner
    return half + half * jnp.tanh(slope)


def nt_dot(left, right):
    return lax.dot_general(
        left, right, (((1,), (1,)), ((), ())), preferred_element_type=jnp.float32
    )


def velocity_kernel(
    side_ref,
    hidden_hbm,
    modulation_ref,
    in_weight_hbm,
    in_bias_ref,
    out_weight_hbm,
    out_bias_ref,
    mel_weight_ref,
    mel_bias_ref,
    noisy_ref,
    holder_ref,
    position_ref,
    own_ref,
    sent_ref,
    base_ref,
    hidden_ref,
    in_weight_ref,
    out_weight_ref,
    mel_pad_ref,
    bias_pad_ref,
    tall_ref,
    normed_ref,
    active_ref,
    speed_ref,
    back_ref,
    hidden_sem,
    in_sem,
    out_sem,
    *,
    block,
    tail,
    in_chunk,
):
    frames, width = hidden_ref.shape
    units = in_weight_ref.shape[1]
    half_rows = frames // 2
    mel_bins = noisy_ref.shape[0]
    chips = own_ref.shape[0] // GROUP
    f32, bf16 = jnp.float32, jnp.bfloat16
    hidden_copies = []
    for i in range(frames // block):
        rows = pl.ds(i * block, block)
        copy = pltpu.make_async_copy(
            hidden_hbm.at[0, rows, :], hidden_ref.at[rows, :], hidden_sem.at[i]
        )
        copy.start()
        hidden_copies.append(copy)
    in_copies = []
    for i in range(units // in_chunk):
        columns = pl.ds(i * in_chunk, in_chunk)
        copy = pltpu.make_async_copy(
            in_weight_hbm.at[:, columns], in_weight_ref.at[:, columns], in_sem.at[i]
        )
        copy.start()
        in_copies.append(copy)
    out_copy = pltpu.make_async_copy(out_weight_hbm, out_weight_ref, out_sem)
    out_copy.start()

    def spaced_store(ref, first, values):
        for i in range(values.shape[0] // chips):
            ref[pl.ds(first + i, chips, stride=GROUP), :] = values[i * chips : (i + 1) * chips, :]

    used = half_rows // chips
    blank = jnp.zeros(((GROUP - used) * chips, LANES), f32)
    half = pl.ds(pl.multiple_of(side_ref[0] * half_rows, half_rows), half_rows)
    tall_ref[...] = jnp.zeros(tall_ref.shape, f32)
    tall_ref[:mel_bins, :] = noisy_ref[:, half]
    for i in range(half_rows // LANES):
        row = pl.ds(side_ref[0] * (half_rows // LANES) + i, 1)
        columns = slice(i * LANES, (i + 1) * LANES)
        tall_ref[mel_bins : mel_bins + 1, columns] = holder_ref[row, :].astype(f32)
        tall_ref[mel_bins + 1 : mel_bins + 2, columns] = jnp.where(
            position_ref[row, :] == 0, 1.0, 0.0
        )
    spaced_store(base_ref, 0, tall_ref[...].T)
    spaced_store(base_ref, used, blank)
    spaced_store(speed_ref.at[0], used, blank)
    spaced_store(speed_ref.at[1], used, blank)
    mel_pad_ref[...] = jnp.zeros(mel_pad_ref.shape, bf16)
    mel_pad_ref[:mel_bins, :] = mel_weight_ref[...]
    bias_pad_ref[...] = jnp.zeros(bias_pad_ref.shape, f32)
    bias_pad_ref[:, :mel_bins] = mel_bias_ref[...]

    scale = 1.0 + modulation_ref[1:2, :]
    for i in range(frames // block):
        hidden_copies[i].wait()
        for low in range(i * block, (i + 1) * block, 64):
            rows = slice(low, low + 64)
            normed = layer_norm(hidden_ref[rows, :].astype(f32)) * scale + modulation_ref[0:1, :]
            normed_ref[rows, :] = normed.astype(bf16)

    for j in range(units // in_chunk):
        columns = slice(j * in_chunk, (j + 1) * in_chunk)
        in_copies[j].wait()
        for i in range(frames // block):
            rows = slice(i * block, (i + 1) * block)
            inner = jnp.dot(
                normed_ref[rows, :], in_weight_ref[:, columns], preferred_element_type=f32
            )
            active_ref[rows, columns] = gelu_tanh(inner + in_bias_ref[:, columns]).astype(bf16)

    out_copy.wait()
    out_scale = 1.0 + modulation_ref[4:5, :]

    def finish(i):
        for low in range(i * tail, (i + 1) * tail, 64):
            rows = slice(low, low + 64)
            back = back_ref[i % 2, low - i * tail : low - i * tail + 64, :] + out_bias_ref[...]
            block_out = hidden_ref[rows, :].astype(f32) + modulation_ref[2:3, :] * back
            final = layer_norm(block_out) * out_scale + modulation_ref[3:4, :]
            normed_ref[rows, :] = final.astype(bf16)

    def emit(i):
        first = i * tail
        speed = nt_dot(normed_ref[first : first + tail, :], mel_pad_ref[...]) + bias_pad_ref[...]
        part = first // half_rows
        spaced_store(speed_ref.at[part], (first - part * half_rows) // chips, speed)

    count = frames // tail
    for i in range(count + 1):
        if i < count:
            back_ref[i % 2] = jnp.dot(
                active_ref[i * tail : (i + 1) * tail, :],
                out_weight_ref[...],
                preferred_element_type=f32,
            )
        if i > 0:
            finish(i - 1)
            emit(i - 1)

    @pl.when(side_ref[0] == 0)
    def _():
        own_ref[...] = speed_ref[0]
        sent_ref[...] = speed_ref[1]

    @pl.when(side_ref[0] != 0)
    def _():
        own_ref[...] = speed_ref[1]
        sent_ref[...] = speed_ref[0]


def velocity_halves(
    side,
    hidden,
    modulation,
    feedforward_in_weight,
    feedforward_in_bias,
    feedforward_out_weight,
    feedforward_out_bias,
    mel_velocity_weight,
    mel_velocity_bias,
    noisy_mel_state,
    frame_holder,
    frame_position,
    chips,
    block=384,
    tail=384,
    in_chunk=1024,
):
    frames, width = hidden.shape[1:]
    units = feedforward_in_weight.shape[1]
    f32, bf16 = jnp.float32, jnp.bfloat16
    spaced = jax.ShapeDtypeStruct((chips * GROUP, LANES), f32)
    vmem = pl.BlockSpec(memory_space=pltpu.VMEM)
    hbm = pl.BlockSpec(memory_space=pl.ANY)
    return pl.pallas_call(
        functools.partial(velocity_kernel, block=block, tail=tail, in_chunk=in_chunk),
        out_shape=(spaced,) * 3,
        in_specs=[pl.BlockSpec(memory_space=pltpu.SMEM), hbm, vmem, hbm, vmem, hbm] + [vmem] * 6,
        out_specs=(vmem,) * 3,
        scratch_shapes=[
            pltpu.VMEM((frames, width), bf16),
            pltpu.VMEM((width, units), bf16),
            pltpu.VMEM((units, width), bf16),
            pltpu.VMEM((LANES, width), bf16),
            pltpu.VMEM((1, LANES), f32),
            pltpu.VMEM((LANES, frames // 2), f32),
            pltpu.VMEM((frames, width), bf16),
            pltpu.VMEM((frames, units), bf16),
            pltpu.VMEM((2, chips * GROUP, LANES), f32),
            pltpu.VMEM((2, tail, width), f32),
            pltpu.SemaphoreType.DMA((frames // block,)),
            pltpu.SemaphoreType.DMA((units // in_chunk,)),
            pltpu.SemaphoreType.DMA(()),
        ],
        compiler_params=pltpu.CompilerParams(vmem_limit_bytes=60 * 1024 * 1024),
        name="velocity",
    )(
        side,
        hidden,
        modulation,
        feedforward_in_weight,
        feedforward_in_bias[None],
        feedforward_out_weight,
        feedforward_out_bias[None],
        mel_velocity_weight.T,
        mel_velocity_bias[None],
        noisy_mel_state,
        frame_holder.reshape(-1, LANES),
        frame_position.reshape(-1, LANES),
    )


SIN_TERMS = (
    3.141592579805583,
    -5.167706866168128,
    2.550031193522954,
    -0.5980441939334223,
    0.07721838619602994,
)


def snake_rows(signal, turns, inverse):
    half_turns = signal * turns
    part = half_turns - jnp.round(half_turns)
    square = part * part
    poly = SIN_TERMS[4] * square + SIN_TERMS[3]
    poly = poly * square + SIN_TERMS[2]
    poly = poly * square + SIN_TERMS[1]
    poly = poly * square + SIN_TERMS[0]
    sine = poly * part
    return signal + sine * sine * inverse


def vocoder_kernel(
    length_ref,
    arrived_ref,
    input_weight_ref,
    input_bias_ref,
    up_weight_hbm,
    up_bias_ref,
    freq_first_ref,
    dilated_weight_ref,
    dilated_bias_ref,
    freq_second_ref,
    second_weight_ref,
    second_bias_ref,
    wave_hbm,
    mel_ref,
    taps_ref,
    shift_wide_ref,
    pre_ref,
    shift_ref,
    up_ref,
    first_ref,
    second_ref,
    out_ref,
    up_weight_ref,
    up_sem,
    even_ref,
    odd_ref,
    wave_ref,
    wave_sem,
    *,
    mel_bins,
    block,
):
    frames = up_ref.shape[1]
    part_rows = arrived_ref.shape[0] // 2
    blocks = frames // block
    halo = 8
    f32, bf16 = jnp.float32, jnp.bfloat16
    length = length_ref[0]

    def keep_rows(first, count):
        row = lax.broadcasted_iota(jnp.int32, (count, 1), 0) + first
        return row < length

    up_copy = pltpu.make_async_copy(up_weight_hbm, up_weight_ref, up_sem)
    up_copy.start()
    arrived = arrived_ref[...]

    def shard_row(shape, axis):
        i = lax.broadcasted_iota(jnp.int32, shape, axis)
        side = (i >= part_rows).astype(jnp.int32)
        inner = i - side * part_rows
        turn = lax.rem(inner, GROUP)
        row = side * (frames // 2) + turn * (part_rows // GROUP) + inner // GROUP
        return jnp.where(turn < frames * GROUP // (2 * part_rows), row, -4 * frames)

    lane = lax.broadcasted_iota(jnp.int32, arrived.shape, 1)
    flagged = jnp.where(lane == mel_bins + 1, arrived.astype(f32), 0.0)
    start = jnp.sum(
        jnp.where(flagged > 0.5, shard_row(arrived.shape, 0).astype(f32), 0.0), keepdims=True
    ).astype(jnp.int32)
    mel_ref[...] = jnp.zeros(mel_ref.shape, f32)
    turned = shard_row((1, arrived.shape[0]), 1) - start
    for i in range(frames // 128):
        ahead = turned - i * 128 - lax.broadcasted_iota(jnp.int32, (128, 1), 0)
        pick = ((ahead == 0) | (ahead == -frames)).astype(bf16)
        mel_ref[halo + i * 128 : halo + (i + 1) * 128, :] = jnp.dot(
            pick, arrived, preferred_element_type=f32
        )
    for k in range(KPRE):
        low = halo + k - KPRE // 2
        taps_ref[:, k * LANES : (k + 1) * LANES] = mel_ref[low : low + frames, :].astype(bf16)
    shift_wide_ref[...] = jnp.zeros(shift_wide_ref.shape, f32)
    for i in range(blocks):
        rows = slice(i * block, (i + 1) * block)
        pre = jnp.dot(taps_ref[rows, :], input_weight_ref[...], preferred_element_type=f32)
        pre = jnp.where(keep_rows(i * block, block), pre + input_bias_ref[...], 0.0)
        shift_wide_ref[halo + i * block : halo + (i + 1) * block, :] = pre
    for k in range(3):
        low = halo + k - 1
        pre_ref[k] = shift_wide_ref[low : low + frames, :].astype(bf16)
    shift_ref[...] = jnp.zeros(shift_ref.shape, f32)

    turns_first = freq_first_ref[...] * (1.0 / math.pi)
    inverse_first = 1.0 / freq_first_ref[...]
    turns_second = freq_second_ref[...] * (1.0 / math.pi)
    inverse_second = 1.0 / freq_second_ref[...]

    def neighbour_rows(offset):
        low = halo + offset
        return shift_ref[low : low + frames, :].astype(bf16)

    up_copy.wait()

    def pipeline(product, finish):
        for i in range(blocks):
            rows = slice(i * block, (i + 1) * block)
            even_ref[rows, :] = product(0, rows)

        for r in range(UP):
            ready_ref, next_ref = (even_ref, odd_ref) if r % 2 == 0 else (odd_ref, even_ref)
            for i in range(blocks):
                rows = slice(i * block, (i + 1) * block)
                if r + 1 < UP:
                    next_ref[rows, :] = product(r + 1, rows)
                for low in range(i * block, (i + 1) * block, 64):
                    finish(r, low, ready_ref[low : low + 64, :])

    def up_product(r, rows):
        side = 0 if r < UP // 2 else 2
        return jnp.dot(
            jnp.concatenate([pre_ref[1, rows, :], pre_ref[side, rows, :]], axis=1),
            jnp.concatenate(
                [up_weight_ref[r + UP // 2], up_weight_ref[(r + UP // 2 + UP) % KT]],
                axis=0,
            ),
            preferred_element_type=f32,
        )

    def up_finish(r, low, up):
        rows = slice(low, low + 64)
        up = jnp.where(keep_rows(low, 64), up + up_bias_ref[...], 0.0)
        up = up.astype(bf16)
        up_ref[r, rows, :] = up
        first = snake_rows(up.astype(f32), turns_first, inverse_first)
        first_ref[r + 3, rows, :] = first.astype(bf16)

    pipeline(up_product, up_finish)

    for r in range(DILATION_RATE):
        shift_ref[halo : halo + frames, :] = first_ref[r + 3].astype(f32)
        first_ref[r + 3 + UP] = neighbour_rows(1)
    for r in range(UP - DILATION_RATE, UP):
        shift_ref[halo : halo + frames, :] = first_ref[r + 3].astype(f32)
        first_ref[r + 3 - UP] = neighbour_rows(-1)

    def inner_product(r, rows):
        around = [first_ref[r + DILATION_RATE * k, rows, :] for k in range(3)]
        return jnp.dot(
            jnp.concatenate(around, axis=1),
            dilated_weight_ref[...],
            preferred_element_type=f32,
        )

    def inner_finish(r, low, inner):
        inner = jnp.where(keep_rows(low, 64), inner + dilated_bias_ref[...], 0.0)
        second = snake_rows(inner, turns_second, inverse_second)
        second_ref[r + 1, low : low + 64, :] = second.astype(bf16)

    pipeline(inner_product, inner_finish)

    shift_ref[halo : halo + frames, :] = second_ref[1].astype(f32)
    second_ref[UP + 1] = neighbour_rows(1)
    shift_ref[halo : halo + frames, :] = second_ref[UP].astype(f32)
    second_ref[0] = neighbour_rows(-1)

    narrow = 256 // UP
    row = lax.broadcasted_iota(jnp.int32, (256, 256), 0)
    col = lax.broadcasted_iota(jnp.int32, (256, 256), 1)
    weave = (col == lax.rem(row, narrow) * UP + row // narrow).astype(bf16)

    def outer_product(low):
        for r in range(UP):
            around = [second_ref[r + k, low : low + 128, :] for k in range(3)]
            outer = jnp.dot(
                jnp.concatenate(around, axis=1),
                second_weight_ref[...],
                preferred_element_type=f32,
            )
            outer = jnp.where(keep_rows(low, 128), outer + second_bias_ref[...], 0.0)
            up = up_ref[r, low : low + 128, :].astype(f32)
            out_ref[r, low : low + 128, :] = (up + outer).astype(bf16)

    copies = []

    def woven(low):
        for first in range(low, low + 128, narrow):
            phases = jnp.concatenate(
                [out_ref[r, first : first + narrow, :] for r in range(UP)], axis=0
            )
            samples = lax.dot_general(
                phases, weave, (((0,), (0,)), ((), ())), preferred_element_type=f32
            )
            wave_ref[:, first * UP : (first + narrow) * UP] = samples.astype(bf16)
        columns = pl.ds(low * UP, 128 * UP)
        copy = pltpu.make_async_copy(
            wave_ref.at[:, columns], wave_hbm.at[0, :, columns], wave_sem.at[low // 128]
        )
        copy.start()
        copies.append(copy)

    for low in range(0, frames + 128, 128):
        if low < frames:
            outer_product(low)
        if low > 0:
            woven(low - 128)
    for copy in copies:
        copy.wait()


def vocoder(
    arrived,
    length,
    mel_bins,
    input_conv_weight,
    input_conv_bias,
    transposed_conv_weight,
    transposed_conv_bias,
    snake_freq_first,
    dilated_conv_weight,
    dilated_conv_bias,
    snake_freq_second,
    second_conv_weight,
    second_conv_bias,
    frames,
    block=128,
):
    wide = input_conv_bias.shape[0]
    channels = transposed_conv_bias.shape[0]
    f32, bf16 = jnp.float32, jnp.bfloat16
    taps_weight = jnp.pad(
        input_conv_weight.reshape(KPRE, mel_bins, wide), ((0, 0), (0, LANES - mel_bins), (0, 0))
    ).reshape(KPRE * LANES, wide)
    operands = [
        arrived,
        taps_weight,
        input_conv_bias[None],
        transposed_conv_weight.reshape(KT, channels, wide).transpose(0, 2, 1),
        transposed_conv_bias[None],
        snake_freq_first[None],
        dilated_conv_weight,
        dilated_conv_bias[None],
        snake_freq_second[None],
        second_conv_weight,
        second_conv_bias[None],
    ]
    return pl.pallas_call(
        functools.partial(vocoder_kernel, mel_bins=mel_bins, block=block),
        out_shape=jax.ShapeDtypeStruct((1, channels, frames * UP), bf16),
        in_specs=[pl.BlockSpec(memory_space=pltpu.SMEM)]
        + [
            pl.BlockSpec(memory_space=pl.ANY)
            if x.ndim == 3 and x.shape[0] == KT
            else pl.BlockSpec(memory_space=pltpu.VMEM)
            for x in operands
        ],
        out_specs=pl.BlockSpec(memory_space=pl.ANY),
        scratch_shapes=[
            pltpu.VMEM((frames + 16, LANES), f32),
            pltpu.VMEM((frames, KPRE * LANES), bf16),
            pltpu.VMEM((frames + 16, wide), f32),
            pltpu.VMEM((3, frames, wide), bf16),
            pltpu.VMEM((frames + 16, channels), f32),
            pltpu.VMEM((UP, frames, channels), bf16),
            pltpu.VMEM((UP + 6, frames, channels), bf16),
            pltpu.VMEM((UP + 2, frames, channels), bf16),
            pltpu.VMEM((UP, frames, channels), bf16),
            pltpu.VMEM((KT, wide, channels), bf16),
            pltpu.SemaphoreType.DMA(()),
            pltpu.VMEM((frames, channels), f32),
            pltpu.VMEM((frames, channels), f32),
            pltpu.VMEM((channels, frames * UP), bf16),
            pltpu.SemaphoreType.DMA((frames // 128,)),
        ],
        compiler_params=pltpu.CompilerParams(vmem_limit_bytes=50 * 1024 * 1024),
        name="vocoder",
    )(length, *operands)


def local(
    hidden,
    noisy_mel_state,
    modulation,
    feedforward_in_weight,
    feedforward_in_bias,
    feedforward_out_weight,
    feedforward_out_bias,
    mel_velocity_weight,
    mel_velocity_bias,
    input_conv_weight,
    input_conv_bias,
    transposed_conv_weight,
    transposed_conv_bias,
    snake_freq_first,
    dilated_conv_weight,
    dilated_conv_bias,
    snake_freq_second,
    second_conv_weight,
    second_conv_bias,
    frame_holder,
    frame_position,
    holder_utterance_length,
):
    step_size = math.cos(0.5 * math.pi * (NFE - 1) / NFE)
    chips = lax.axis_size("seq")
    owners = lax.axis_size("branch") * chips
    mel_bins, frames = noisy_mel_state.shape
    branch_side = lax.axis_index("branch").astype(jnp.int32)
    own_half, sent_half, base = velocity_halves(
        branch_side[None],
        hidden,
        modulation,
        feedforward_in_weight,
        feedforward_in_bias,
        feedforward_out_weight,
        feedforward_out_bias,
        mel_velocity_weight,
        mel_velocity_bias,
        noisy_mel_state,
        frame_holder,
        frame_position,
        chips,
    )
    peer_half = lax.ppermute(sent_half, "branch", [(0, 1), (1, 0)])
    conditional = jnp.where(branch_side == 0, own_half, peer_half)
    unconditional = jnp.where(branch_side == 0, peer_half, own_half)
    guided = (1.0 + GUIDE) * conditional - GUIDE * unconditional
    packed = (base + step_size * guided).astype(jnp.bfloat16)
    spread = lax.all_to_all(packed.reshape(chips, GROUP, LANES), "seq", 0, 0, tiled=True)
    rows = spread.reshape(chips * GROUP, LANES)
    owner_of = rows[:, mel_bins].astype(jnp.int32)
    slot_of = owner_of * GROUP + jnp.arange(chips * GROUP, dtype=jnp.int32) % GROUP
    onehot = (slot_of[:, None] == jnp.arange(owners * GROUP, dtype=jnp.int32)[None, :]).astype(
        jnp.bfloat16
    )
    slots = lax.dot_general(
        onehot, rows, (((0,), (0,)), ((), ())), preferred_element_type=jnp.float32
    ).astype(jnp.bfloat16)
    arrived = lax.all_to_all(
        slots.reshape(owners, GROUP, LANES), ("branch", "seq"), 0, 0, tiled=True
    ).reshape(owners * GROUP, LANES)
    self_owner = lax.axis_index(("branch", "seq"))
    length = lax.dynamic_slice_in_dim(holder_utterance_length, self_owner, 1, 0)
    return vocoder(
        arrived,
        length,
        mel_bins,
        input_conv_weight,
        input_conv_bias,
        transposed_conv_weight,
        transposed_conv_bias,
        snake_freq_first,
        dilated_conv_weight,
        dilated_conv_bias,
        snake_freq_second,
        second_conv_weight,
        second_conv_bias,
        frames,
    )


def solution(mesh):
    return jax.shard_map(
        local,
        mesh=mesh,
        in_specs=(
            P("branch", "seq", None),
            P(None, "seq"),
            P(),
            P(),
            P(),
            P(),
            P(),
            P(),
            P(),
            P(),
            P(),
            P(),
            P(),
            P(),
            P(),
            P(),
            P(),
            P(),
            P(),
            P("seq"),
            P("seq"),
            P(),
        ),
        out_specs=P(("branch", "seq"), None, None),
        check_vma=False,
    )
```

```python
import functools
import math

import jax
import jax.numpy as jnp
from jax import lax
from jax.experimental import pallas as pl
from jax.experimental.pallas import tpu as pltpu
from jax.sharding import PartitionSpec as P

UP = 8
KT = 16
KPRE = 7
DILATION_RATE = 3
NFE = 16


GUIDE = 2.0
LANES = 128
GROUP = 8
GELU_SCALE = math.sqrt(2.0 / math.pi)


def layer_norm(row_block):
    row_mean = jnp.mean(row_block, axis=-1, keepdims=True)
    centred = row_block - row_mean
    row_var = jnp.mean(centred * centred, axis=-1, keepdims=True)
    return centred * lax.rsqrt(row_var + 1e-06)


def gelu_tanh(inner):
    slope = inner * (GELU_SCALE + (GELU_SCALE * 0.044715) * (inner * inner))
    half = 0.5 * inner
    return half + half * jnp.tanh(slope)


def nt_dot(left, right):
    return lax.dot_general(
        left, right, (((1,), (1,)), ((), ())), preferred_element_type=jnp.float32
    )


def velocity_kernel(
    side_ref,
    hidden_hbm,
    modulation_ref,
    in_weight_hbm,
    in_bias_ref,
    out_weight_hbm,
    out_bias_ref,
    mel_weight_ref,
    mel_bias_ref,
    noisy_ref,
    holder_ref,
    position_ref,
    own_ref,
    sent_ref,
    hidden_ref,
    in_weight_ref,
    out_weight_ref,
    mel_pad_ref,
    bias_pad_ref,
    tall_ref,
    normed_ref,
    active_ref,
    speed_ref,
    back_ref,
    base_ref,
    hidden_sem,
    in_sem,
    out_sem,
    *,
    block,
    tail,
    in_chunk,
):
    frames, width = hidden_ref.shape
    units = in_weight_ref.shape[1]
    half_rows = frames // 2
    mel_bins = noisy_ref.shape[0]
    chips = own_ref.shape[0] // GROUP
    f32, bf16 = jnp.float32, jnp.bfloat16
    hidden_copies = []
    for i in range(frames // block):
        rows = pl.ds(i * block, block)
        copy = pltpu.make_async_copy(
            hidden_hbm.at[0, rows, :], hidden_ref.at[rows, :], hidden_sem.at[i]
        )
        copy.start()
        hidden_copies.append(copy)
    in_copies = []
    for i in range(units // in_chunk):
        columns = pl.ds(i * in_chunk, in_chunk)
        copy = pltpu.make_async_copy(
            in_weight_hbm.at[:, columns], in_weight_ref.at[:, columns], in_sem.at[i]
        )
        copy.start()
        in_copies.append(copy)
    out_copy = pltpu.make_async_copy(out_weight_hbm, out_weight_ref, out_sem)
    out_copy.start()

    def spaced_store(ref, first, values):
        for i in range(values.shape[0] // chips):
            ref[pl.ds(first + i, chips, stride=GROUP), :] = values[i * chips : (i + 1) * chips, :]

    used = half_rows // chips
    blank = jnp.zeros(((GROUP - used) * chips, LANES), f32)
    half = pl.ds(pl.multiple_of(side_ref[0] * half_rows, half_rows), half_rows)
    tall_ref[...] = jnp.zeros(tall_ref.shape, f32)
    tall_ref[:mel_bins, :] = noisy_ref[:, half]
    for i in range(half_rows // LANES):
        row = pl.ds(side_ref[0] * (half_rows // LANES) + i, 1)
        columns = slice(i * LANES, (i + 1) * LANES)
        tall_ref[mel_bins : mel_bins + 1, columns] = holder_ref[row, :].astype(f32)
        tall_ref[mel_bins + 1 : mel_bins + 2, columns] = jnp.where(
            position_ref[row, :] == 0, 1.0, 0.0
        )
    spaced_store(base_ref, 0, tall_ref[...].T)
    spaced_store(base_ref, used, blank)
    spaced_store(speed_ref.at[0], used, blank)
    spaced_store(speed_ref.at[1], used, blank)
    mel_pad_ref[...] = jnp.zeros(mel_pad_ref.shape, bf16)
    mel_pad_ref[:mel_bins, :] = mel_weight_ref[...]
    bias_pad_ref[...] = jnp.zeros(bias_pad_ref.shape, f32)
    bias_pad_ref[:, :mel_bins] = mel_bias_ref[...]

    scale = 1.0 + modulation_ref[1:2, :]
    for i in range(frames // block):
        hidden_copies[i].wait()
        for low in range(i * block, (i + 1) * block, 64):
            rows = slice(low, low + 64)
            normed = layer_norm(hidden_ref[rows, :].astype(f32)) * scale + modulation_ref[0:1, :]
            normed_ref[rows, :] = normed.astype(bf16)

    for j in range(units // in_chunk):
        columns = slice(j * in_chunk, (j + 1) * in_chunk)
        in_copies[j].wait()
        for i in range(frames // block):
            rows = slice(i * block, (i + 1) * block)
            inner = jnp.dot(
                normed_ref[rows, :], in_weight_ref[:, columns], preferred_element_type=f32
            )
            active_ref[rows, columns] = gelu_tanh(inner + in_bias_ref[:, columns]).astype(bf16)

    out_copy.wait()
    out_scale = 1.0 + modulation_ref[4:5, :]

    def finish(i):
        for low in range(i * tail, (i + 1) * tail, 64):
            rows = slice(low, low + 64)
            back = back_ref[i % 2, low - i * tail : low - i * tail + 64, :] + out_bias_ref[...]
            block_out = hidden_ref[rows, :].astype(f32) + modulation_ref[2:3, :] * back
            final = layer_norm(block_out) * out_scale + modulation_ref[3:4, :]
            normed_ref[rows, :] = final.astype(bf16)

    def emit(i):
        first = i * tail
        speed = nt_dot(normed_ref[first : first + tail, :], mel_pad_ref[...]) + bias_pad_ref[...]
        part = first // half_rows
        spaced_store(speed_ref.at[part], (first - part * half_rows) // chips, speed)

    count = frames // tail
    for i in range(count + 1):
        if i < count:
            back_ref[i % 2] = jnp.dot(
                active_ref[i * tail : (i + 1) * tail, :],
                out_weight_ref[...],
                preferred_element_type=f32,
            )
        if i > 0:
            finish(i - 1)
            emit(i - 1)

    step_size = math.cos(0.5 * math.pi * (NFE - 1) / NFE)

    @pl.when(side_ref[0] == 0)
    def _():
        own_ref[...] = base_ref[...] + (step_size * (1.0 + GUIDE)) * speed_ref[0]
        sent_ref[...] = speed_ref[1]

    @pl.when(side_ref[0] != 0)
    def _():
        own_ref[...] = base_ref[...] - (step_size * GUIDE) * speed_ref[1]
        sent_ref[...] = speed_ref[0]


def velocity_halves(
    side,
    hidden,
    modulation,
    feedforward_in_weight,
    feedforward_in_bias,
    feedforward_out_weight,
    feedforward_out_bias,
    mel_velocity_weight,
    mel_velocity_bias,
    noisy_mel_state,
    frame_holder,
    frame_position,
    chips,
    block=384,
    tail=384,
    in_chunk=1024,
):
    frames, width = hidden.shape[1:]
    units = feedforward_in_weight.shape[1]
    f32, bf16 = jnp.float32, jnp.bfloat16
    spaced = jax.ShapeDtypeStruct((chips * GROUP, LANES), f32)
    vmem = pl.BlockSpec(memory_space=pltpu.VMEM)
    hbm = pl.BlockSpec(memory_space=pl.ANY)
    return pl.pallas_call(
        functools.partial(velocity_kernel, block=block, tail=tail, in_chunk=in_chunk),
        out_shape=(spaced,) * 2,
        in_specs=[pl.BlockSpec(memory_space=pltpu.SMEM), hbm, vmem, hbm, vmem, hbm] + [vmem] * 6,
        out_specs=(vmem,) * 2,
        scratch_shapes=[
            pltpu.VMEM((frames, width), bf16),
            pltpu.VMEM((width, units), bf16),
            pltpu.VMEM((units, width), bf16),
            pltpu.VMEM((LANES, width), bf16),
            pltpu.VMEM((1, LANES), f32),
            pltpu.VMEM((LANES, frames // 2), f32),
            pltpu.VMEM((frames, width), bf16),
            pltpu.VMEM((frames, units), bf16),
            pltpu.VMEM((2, chips * GROUP, LANES), f32),
            pltpu.VMEM((2, tail, width), f32),
            pltpu.VMEM((chips * GROUP, LANES), f32),
            pltpu.SemaphoreType.DMA((frames // block,)),
            pltpu.SemaphoreType.DMA((units // in_chunk,)),
            pltpu.SemaphoreType.DMA(()),
        ],
        compiler_params=pltpu.CompilerParams(vmem_limit_bytes=60 * 1024 * 1024),
        name="velocity",
    )(
        side,
        hidden,
        modulation,
        feedforward_in_weight,
        feedforward_in_bias[None],
        feedforward_out_weight,
        feedforward_out_bias[None],
        mel_velocity_weight.T,
        mel_velocity_bias[None],
        noisy_mel_state,
        frame_holder.reshape(-1, LANES),
        frame_position.reshape(-1, LANES),
    )


SIN_TERMS = (
    3.141592579805583,
    -5.167706866168128,
    2.550031193522954,
    -0.5980441939334223,
    0.07721838619602994,
)


def snake_rows(signal, turns, inverse):
    half_turns = signal * turns
    part = half_turns - jnp.round(half_turns)
    square = part * part
    poly = SIN_TERMS[4] * square + SIN_TERMS[3]
    poly = poly * square + SIN_TERMS[2]
    poly = poly * square + SIN_TERMS[1]
    poly = poly * square + SIN_TERMS[0]
    sine = poly * part
    return signal + sine * sine * inverse


def vocoder_kernel(
    length_ref,
    arrived_ref,
    input_weight_ref,
    input_bias_ref,
    up_weight_hbm,
    up_bias_ref,
    freq_first_ref,
    dilated_weight_ref,
    dilated_bias_ref,
    freq_second_ref,
    second_weight_ref,
    second_bias_ref,
    wave_hbm,
    mel_ref,
    taps_ref,
    shift_wide_ref,
    pre_ref,
    shift_ref,
    up_ref,
    first_ref,
    second_ref,
    out_ref,
    up_weight_ref,
    up_sem,
    even_ref,
    odd_ref,
    wave_ref,
    wave_sem,
    *,
    mel_bins,
    block,
):
    frames = up_ref.shape[1]
    part_rows = arrived_ref.shape[0] // 2
    blocks = frames // block
    halo = 8
    f32, bf16 = jnp.float32, jnp.bfloat16
    length = length_ref[0]

    def keep_rows(first, count):
        row = lax.broadcasted_iota(jnp.int32, (count, 1), 0) + first
        return row < length

    up_copy = pltpu.make_async_copy(up_weight_hbm, up_weight_ref, up_sem)
    up_copy.start()
    arrived = arrived_ref[...]

    def shard_row(shape, axis):
        i = lax.broadcasted_iota(jnp.int32, shape, axis)
        side = (i >= part_rows).astype(jnp.int32)
        inner = i - side * part_rows
        turn = lax.rem(inner, GROUP)
        row = side * (frames // 2) + turn * (part_rows // GROUP) + inner // GROUP
        return jnp.where(turn < frames * GROUP // (2 * part_rows), row, -4 * frames)

    lane = lax.broadcasted_iota(jnp.int32, arrived.shape, 1)
    flagged = jnp.where(lane == mel_bins + 1, arrived.astype(f32), 0.0)
    start = jnp.sum(
        jnp.where(flagged > 0.5, shard_row(arrived.shape, 0).astype(f32), 0.0), keepdims=True
    ).astype(jnp.int32)
    mel_ref[...] = jnp.zeros(mel_ref.shape, f32)
    turned = shard_row((1, arrived.shape[0]), 1) - start
    for i in range(frames // 128):
        ahead = turned - i * 128 - lax.broadcasted_iota(jnp.int32, (128, 1), 0)
        pick = ((ahead == 0) | (ahead == -frames)).astype(bf16)
        mel_ref[halo + i * 128 : halo + (i + 1) * 128, :] = jnp.dot(
            pick, arrived, preferred_element_type=f32
        )
    for k in range(KPRE):
        low = halo + k - KPRE // 2
        taps_ref[:, k * LANES : (k + 1) * LANES] = mel_ref[low : low + frames, :].astype(bf16)
    shift_wide_ref[...] = jnp.zeros(shift_wide_ref.shape, f32)
    for i in range(blocks):
        rows = slice(i * block, (i + 1) * block)
        pre = jnp.dot(taps_ref[rows, :], input_weight_ref[...], preferred_element_type=f32)
        pre = jnp.where(keep_rows(i * block, block), pre + input_bias_ref[...], 0.0)
        shift_wide_ref[halo + i * block : halo + (i + 1) * block, :] = pre
    for k in range(3):
        low = halo + k - 1
        pre_ref[k] = shift_wide_ref[low : low + frames, :].astype(bf16)
    shift_ref[...] = jnp.zeros(shift_ref.shape, f32)

    turns_first = freq_first_ref[...] * (1.0 / math.pi)
    inverse_first = 1.0 / freq_first_ref[...]
    turns_second = freq_second_ref[...] * (1.0 / math.pi)
    inverse_second = 1.0 / freq_second_ref[...]

    def neighbour_rows(offset):
        low = halo + offset
        return shift_ref[low : low + frames, :].astype(bf16)

    up_copy.wait()

    def pipeline(product, finish):
        for i in range(blocks):
            rows = slice(i * block, (i + 1) * block)
            even_ref[rows, :] = product(0, rows)

        for r in range(UP):
            ready_ref, next_ref = (even_ref, odd_ref) if r % 2 == 0 else (odd_ref, even_ref)
            for i in range(blocks):
                rows = slice(i * block, (i + 1) * block)
                if r + 1 < UP:
                    next_ref[rows, :] = product(r + 1, rows)
                for low in range(i * block, (i + 1) * block, 64):
                    finish(r, low, ready_ref[low : low + 64, :])

    def up_product(r, rows):
        side = 0 if r < UP // 2 else 2
        return jnp.dot(
            jnp.concatenate([pre_ref[1, rows, :], pre_ref[side, rows, :]], axis=1),
            jnp.concatenate(
                [up_weight_ref[r + UP // 2], up_weight_ref[(r + UP // 2 + UP) % KT]],
                axis=0,
            ),
            preferred_element_type=f32,
        )

    def up_finish(r, low, up):
        rows = slice(low, low + 64)
        up = jnp.where(keep_rows(low, 64), up + up_bias_ref[...], 0.0)
        up = up.astype(bf16)
        up_ref[r, rows, :] = up
        first = snake_rows(up.astype(f32), turns_first, inverse_first)
        first_ref[r + 3, rows, :] = first.astype(bf16)

    pipeline(up_product, up_finish)

    for r in range(DILATION_RATE):
        shift_ref[halo : halo + frames, :] = first_ref[r + 3].astype(f32)
        first_ref[r + 3 + UP] = neighbour_rows(1)
    for r in range(UP - DILATION_RATE, UP):
        shift_ref[halo : halo + frames, :] = first_ref[r + 3].astype(f32)
        first_ref[r + 3 - UP] = neighbour_rows(-1)

    def inner_product(r, rows):
        around = [first_ref[r + DILATION_RATE * k, rows, :] for k in range(3)]
        return jnp.dot(
            jnp.concatenate(around, axis=1),
            dilated_weight_ref[...],
            preferred_element_type=f32,
        )

    def inner_finish(r, low, inner):
        inner = jnp.where(keep_rows(low, 64), inner + dilated_bias_ref[...], 0.0)
        second = snake_rows(inner, turns_second, inverse_second)
        second_ref[r + 1, low : low + 64, :] = second.astype(bf16)

    pipeline(inner_product, inner_finish)

    shift_ref[halo : halo + frames, :] = second_ref[1].astype(f32)
    second_ref[UP + 1] = neighbour_rows(1)
    shift_ref[halo : halo + frames, :] = second_ref[UP].astype(f32)
    second_ref[0] = neighbour_rows(-1)

    narrow = 256 // UP
    row = lax.broadcasted_iota(jnp.int32, (256, 256), 0)
    col = lax.broadcasted_iota(jnp.int32, (256, 256), 1)
    weave = (col == lax.rem(row, narrow) * UP + row // narrow).astype(bf16)

    def outer_product(low):
        for r in range(UP):
            around = [second_ref[r + k, low : low + 128, :] for k in range(3)]
            outer = jnp.dot(
                jnp.concatenate(around, axis=1),
                second_weight_ref[...],
                preferred_element_type=f32,
            )
            outer = jnp.where(keep_rows(low, 128), outer + second_bias_ref[...], 0.0)
            up = up_ref[r, low : low + 128, :].astype(f32)
            out_ref[r, low : low + 128, :] = (up + outer).astype(bf16)

    copies = []

    def woven(low):
        for first in range(low, low + 128, narrow):
            phases = jnp.concatenate(
                [out_ref[r, first : first + narrow, :] for r in range(UP)], axis=0
            )
            samples = lax.dot_general(
                phases, weave, (((0,), (0,)), ((), ())), preferred_element_type=f32
            )
            wave_ref[:, first * UP : (first + narrow) * UP] = samples.astype(bf16)
        columns = pl.ds(low * UP, 128 * UP)
        copy = pltpu.make_async_copy(
            wave_ref.at[:, columns], wave_hbm.at[0, :, columns], wave_sem.at[low // 128]
        )
        copy.start()
        copies.append(copy)

    for low in range(0, frames + 128, 128):
        if low < frames:
            outer_product(low)
        if low > 0:
            woven(low - 128)
    for copy in copies:
        copy.wait()


def vocoder(
    arrived,
    length,
    mel_bins,
    input_conv_weight,
    input_conv_bias,
    transposed_conv_weight,
    transposed_conv_bias,
    snake_freq_first,
    dilated_conv_weight,
    dilated_conv_bias,
    snake_freq_second,
    second_conv_weight,
    second_conv_bias,
    frames,
    block=128,
):
    wide = input_conv_bias.shape[0]
    channels = transposed_conv_bias.shape[0]
    f32, bf16 = jnp.float32, jnp.bfloat16
    taps_weight = jnp.pad(
        input_conv_weight.reshape(KPRE, mel_bins, wide), ((0, 0), (0, LANES - mel_bins), (0, 0))
    ).reshape(KPRE * LANES, wide)
    operands = [
        arrived,
        taps_weight,
        input_conv_bias[None],
        transposed_conv_weight.reshape(KT, channels, wide).transpose(0, 2, 1),
        transposed_conv_bias[None],
        snake_freq_first[None],
        dilated_conv_weight,
        dilated_conv_bias[None],
        snake_freq_second[None],
        second_conv_weight,
        second_conv_bias[None],
    ]
    return pl.pallas_call(
        functools.partial(vocoder_kernel, mel_bins=mel_bins, block=block),
        out_shape=jax.ShapeDtypeStruct((1, channels, frames * UP), bf16),
        in_specs=[pl.BlockSpec(memory_space=pltpu.SMEM)]
        + [
            pl.BlockSpec(memory_space=pl.ANY)
            if x.ndim == 3 and x.shape[0] == KT
            else pl.BlockSpec(memory_space=pltpu.VMEM)
            for x in operands
        ],
        out_specs=pl.BlockSpec(memory_space=pl.ANY),
        scratch_shapes=[
            pltpu.VMEM((frames + 16, LANES), f32),
            pltpu.VMEM((frames, KPRE * LANES), bf16),
            pltpu.VMEM((frames + 16, wide), f32),
            pltpu.VMEM((3, frames, wide), bf16),
            pltpu.VMEM((frames + 16, channels), f32),
            pltpu.VMEM((UP, frames, channels), bf16),
            pltpu.VMEM((UP + 6, frames, channels), bf16),
            pltpu.VMEM((UP + 2, frames, channels), bf16),
            pltpu.VMEM((UP, frames, channels), bf16),
            pltpu.VMEM((KT, wide, channels), bf16),
            pltpu.SemaphoreType.DMA(()),
            pltpu.VMEM((frames, channels), f32),
            pltpu.VMEM((frames, channels), f32),
            pltpu.VMEM((channels, frames * UP), bf16),
            pltpu.SemaphoreType.DMA((frames // 128,)),
        ],
        compiler_params=pltpu.CompilerParams(vmem_limit_bytes=50 * 1024 * 1024),
        name="vocoder",
    )(length, *operands)


def local(
    hidden,
    noisy_mel_state,
    modulation,
    feedforward_in_weight,
    feedforward_in_bias,
    feedforward_out_weight,
    feedforward_out_bias,
    mel_velocity_weight,
    mel_velocity_bias,
    input_conv_weight,
    input_conv_bias,
    transposed_conv_weight,
    transposed_conv_bias,
    snake_freq_first,
    dilated_conv_weight,
    dilated_conv_bias,
    snake_freq_second,
    second_conv_weight,
    second_conv_bias,
    frame_holder,
    frame_position,
    holder_utterance_length,
):
    step_size = math.cos(0.5 * math.pi * (NFE - 1) / NFE)
    chips = lax.axis_size("seq")
    owners = lax.axis_size("branch") * chips
    mel_bins, frames = noisy_mel_state.shape
    branch_side = lax.axis_index("branch").astype(jnp.int32)
    own_half, sent_half = velocity_halves(
        branch_side[None],
        hidden,
        modulation,
        feedforward_in_weight,
        feedforward_in_bias,
        feedforward_out_weight,
        feedforward_out_bias,
        mel_velocity_weight,
        mel_velocity_bias,
        noisy_mel_state,
        frame_holder,
        frame_position,
        chips,
    )
    peer_half = lax.ppermute(sent_half, "branch", [(0, 1), (1, 0)])
    peer_weight = jnp.where(branch_side == 0, -step_size * GUIDE, step_size * (1.0 + GUIDE))
    packed = (own_half + peer_weight * peer_half).astype(jnp.bfloat16)
    spread = lax.all_to_all(packed.reshape(chips, GROUP, LANES), "seq", 0, 0, tiled=True)
    rows = spread.reshape(chips * GROUP, LANES)
    owner_of = rows[:, mel_bins].astype(jnp.int32)
    slot_of = owner_of * GROUP + jnp.arange(chips * GROUP, dtype=jnp.int32) % GROUP
    onehot = (slot_of[:, None] == jnp.arange(owners * GROUP, dtype=jnp.int32)[None, :]).astype(
        jnp.bfloat16
    )
    slots = lax.dot_general(
        onehot, rows, (((0,), (0,)), ((), ())), preferred_element_type=jnp.float32
    ).astype(jnp.bfloat16)
    arrived = lax.all_to_all(
        slots.reshape(owners, GROUP, LANES), ("branch", "seq"), 0, 0, tiled=True
    ).reshape(owners * GROUP, LANES)
    self_owner = lax.axis_index(("branch", "seq"))
    length = lax.dynamic_slice_in_dim(holder_utterance_length, self_owner, 1, 0)
    return vocoder(
        arrived,
        length,
        mel_bins,
        input_conv_weight,
        input_conv_bias,
        transposed_conv_weight,
        transposed_conv_bias,
        snake_freq_first,
        dilated_conv_weight,
        dilated_conv_bias,
        snake_freq_second,
        second_conv_weight,
        second_conv_bias,
        frames,
    )


def solution(mesh):
    return jax.shard_map(
        local,
        mesh=mesh,
        in_specs=(
            P("branch", "seq", None),
            P(None, "seq"),
            P(),
            P(),
            P(),
            P(),
            P(),
            P(),
            P(),
            P(),
            P(),
            P(),
            P(),
            P(),
            P(),
            P(),
            P(),
            P(),
            P(),
            P("seq"),
            P("seq"),
            P(),
        ),
        out_specs=P(("branch", "seq"), None, None),
        check_vma=False,
    )
```
